256 devices in a mesh: region: 32 (over z, x_hi, core), member: 8 (over y, x_lo).
Axes of the slice: x: 4 (x_hi: 2, x_lo: 2; x = x_hi * 2 + x_lo), y: 4, z: 8, core: 2. Of those that a mesh axis runs over, the one named last changes fastest.
Arguments:
- state: float32 [1024, 256, 256], P('member', 'region'), may hold values from -8 to 8
- neighbours: int32 [256, 5], replicated, may hold values from 0 to 255, as said below
- obs_cell: int32 [256, 2, 64], replicated, may hold values from 0 to 255
- obs_values: float32 [256, 2, 64], replicated, may hold values from -6 to 6
- obs_var: float32 [256, 2, 64], replicated, may hold values from 0.25 to 1
Outputs:
- analysis: float32 [1024, 256, 256], P('member', 'region')
The draws below stay inside these ranges and needn't reach their ends.
Inputs may be any that keep to these rules, and one draw needn't show every extreme that they name: `neighbours`: patch g lies in region g // 8. Each patch lists 5 different patches in some order: two of the region before its own and two of the region after it (regions wrap around), and one other patch of its own region.
All inputs are finite; a program needn't handle non-finite values.
Results may differ from the reference program's by a relative error of at most 0.0003.
Values sent between devices are 32-bit elements; how exact they have to be, the bound alone decides.
A program may use at most 128 MiB of HBM per device.

```python
import math
import jax
import jax.numpy as jnp
from jax import lax

K = 1024
CELLS = 256
OBS = 64
NBR = 5
NBATCH = 2
P_REG = 8
NPATCH = 256


def neighbour_table(key):
    base = jax.random.fold_in(key, 101)
    keys = jax.random.split(base, 6)
    patch = jnp.arange(NPATCH, dtype=jnp.int32)
    regions = NPATCH // P_REG
    region = patch // P_REG
    within = patch % P_REG
    first_prev = jax.random.randint(keys[0], (NPATCH,), 0, P_REG)
    second_prev = (first_prev + 1 + jax.random.randint(keys[1], (NPATCH,), 0, P_REG - 1)) % P_REG
    first_next = jax.random.randint(keys[2], (NPATCH,), 0, P_REG)
    second_next = (first_next + 1 + jax.random.randint(keys[3], (NPATCH,), 0, P_REG - 1)) % P_REG
    same_region = (within + 1 + jax.random.randint(keys[4], (NPATCH,), 0, P_REG - 1)) % P_REG
    before = (region - 1) % regions * P_REG
    after = (region + 1) % regions * P_REG
    own_base = region * P_REG
    columns = jnp.stack([before + first_prev, before + second_prev, after + first_next, after + second_next, own_base + same_region], axis=1)
    orders = jax.vmap(lambda single: jax.random.permutation(single, NBR))(jax.random.split(keys[5], NPATCH))
    return jnp.take_along_axis(columns, orders, axis=1).astype(jnp.int32)


def draw_neighbours(key, part):
    return neighbour_table(key)


def draw_state(key, part):
    table = neighbour_table(key)
    white_key = jax.random.fold_in(key, 23)
    walk_key = jax.random.fold_in(key, 31)
    shared_key = jax.random.fold_in(key, 37)
    norm = jnp.sqrt(jnp.float32(CELLS))
    white = 0.5 * jax.random.normal(white_key, (K, NPATCH, CELLS), jnp.float32)
    steps = jax.random.normal(walk_key, (K, NPATCH, CELLS), jnp.float32)
    shared_steps = jax.random.normal(shared_key, (K, CELLS), jnp.float32)
    walk = jnp.cumsum(steps, axis=2) / norm
    local = walk
    for column in range(NBR):
        local = local + jnp.take(walk, table[:, column], axis=1)
    shared = jnp.cumsum(shared_steps, axis=1) / norm
    field = 2.0 * shared[:, None, :] + 0.5 * local + white
    return jnp.clip(field, -8.0, 8.0)


def set_ends(result, stream_key, low, top_value):
    longest = result.shape.index(max(result.shape))
    spots = []
    for shift in (0, 1):
        where = [jax.random.randint(jax.random.fold_in(stream_key, axis), (), 0, length) for axis, length in enumerate(result.shape)]
        where[longest] = (where[longest] + shift) % result.shape[longest]
        spots.append(tuple(where))
    return result.at[spots[0]].set(low).at[spots[1]].set(top_value)


def scatter_about(own_key, shape, width, bound, kind=jnp.bfloat16):
    result = width * jax.random.normal(own_key, shape, jnp.float32)
    return jnp.clip(result, min=-bound, max=bound).astype(kind)


def setup_inputs(seed: int = 0) -> dict:
    streams_of = jax.random.split(jax.random.key(seed), 6)
    return {
        "state": draw_state(jax.random.fold_in(streams_of[5], 71), 0),
        "neighbours": draw_neighbours(jax.random.fold_in(streams_of[5], 71), 0),
        "obs_cell": set_ends(jax.random.randint(streams_of[2], (NPATCH, NBATCH, OBS), 0, CELLS), jax.random.fold_in(streams_of[2], 1), 0, CELLS - 1).astype(jnp.int32),
        "obs_values": scatter_about(streams_of[3], (NPATCH, NBATCH, OBS), 1.0, 6.0, jnp.float32),
        "obs_var": jnp.clip(jnp.exp(jax.random.uniform(streams_of[4], (NPATCH, NBATCH, OBS), jnp.float32, math.log(0.25), math.log(1.0))), 0.25, 1.0),
    }


HIGHEST = lax.Precision.HIGHEST

def analyse(stacked, values, variances, patch_state):
    members = stacked.shape[1]
    obs_mean = jnp.mean(stacked, axis=1)
    spread = stacked - obs_mean[:, None]
    innovation = values - obs_mean
    covariance = jnp.dot(spread, spread.T, precision=HIGHEST) / (members - 1.0) + jnp.diag(variances)
    state_mean = jnp.mean(patch_state, axis=0)
    anomaly = patch_state - state_mean[None, :]
    cross_cov = jnp.dot(spread, anomaly, precision=HIGHEST)
    factor = jnp.linalg.cholesky(covariance)
    kalman_gain = jax.scipy.linalg.cho_solve((factor, True), cross_cov) / (members - 1.0)
    combined = innovation[:, None] - 0.5 * spread
    update = lax.dot_general(combined, kalman_gain, (((0,), (0,)), ((), ())), precision=HIGHEST)
    return patch_state + update

def reference(state, neighbours, obs_cell, obs_values, obs_var):
    ensemble = jnp.transpose(state, (1, 0, 2))
    widening = jnp.arange(NBR, dtype=jnp.float32) + 2.0
    for batch in range(NBATCH):
        picks = obs_cell[:, batch, :]
        obs_rows = jax.vmap(lambda field, index: field[:, index].T)(ensemble, picks)
        values = obs_values[:, batch, :]
        variances = obs_var[:, batch, :]

        def per_patch(inputs):
            patch, field = inputs
            links = neighbours[patch]
            stacked = jnp.concatenate([obs_rows[patch], obs_rows[links].reshape(NBR * OBS, K)], axis=0)
            wanted = jnp.concatenate([values[patch], values[links].reshape(-1)])
            noise = jnp.concatenate([variances[patch], (variances[links] * widening[:, None]).reshape(-1)])
            return analyse(stacked, wanted, noise, field)
        ensemble = lax.map(per_patch, (jnp.arange(NPATCH, dtype=jnp.int32), ensemble))
    return jnp.transpose(ensemble, (1, 0, 2))
```

```python
import functools

import jax
import jax.numpy as jnp
from jax import lax
from jax.experimental import pallas as pl
from jax.experimental.pallas import tpu as pltpu
from jax.sharding import PartitionSpec as P

F32 = jnp.float32
BF16 = jnp.bfloat16
HIGHEST = lax.Precision.HIGHEST
MESH = pl.DeviceIdType.MESH
TILE = (8, 128)
OBS = 64
VMEM = pl.BlockSpec(memory_space=pltpu.VMEM)
SMEM = pl.BlockSpec(memory_space=pltpu.SMEM)


def dot(a, b, precision=None):
    return lax.dot_general(a, b, (((1,), (0,)), ((), ())), precision=precision, preferred_element_type=F32)


def dot_t(a, b, precision=None):
    return lax.dot_general(a, b, (((1,), (1,)), ((), ())), precision=precision, preferred_element_type=F32)


def split(x):
    high = x.astype(BF16)
    return high, (x - high.astype(F32)).astype(BF16)


def spread_tile(x):
    return jnp.broadcast_to(x, TILE)


def solve8(e, r):
    m = {}
    q = [None] * 8
    for i in range(0, 8, 2):
        a, b, d = e[i][i], e[i + 1][i], e[i + 1][i + 1]
        inv = 1.0 / (a * d - b * b)
        ai, bi, di = d * inv, b * inv, a * inv
        for k in range(i + 2, 8):
            m[k, i] = e[k][i] * ai - e[k][i + 1] * bi
            m[k, i + 1] = e[k][i + 1] * di - e[k][i] * bi
        for k in range(i + 2, 8):
            for j in range(i + 2, k + 1):
                e[k][j] = e[k][j] - (m[k, i] * e[j][i] + m[k, i + 1] * e[j][i + 1])
        for k in range(i + 2, 8):
            r[k] = r[k] - (m[k, i] * r[i] + m[k, i + 1] * r[i + 1])
        q[i], q[i + 1] = ai * r[i] - bi * r[i + 1], di * r[i + 1] - bi * r[i]
    for i in range(6, 0, -2):
        for k in range(i):
            q[k] = q[k] - (m[i, k] * q[i] + m[i + 1, k] * q[i + 1])
    return q


def inverse128(block):
    lane = lax.broadcasted_iota(jnp.int32, TILE, 1)
    sub = lax.broadcasted_iota(jnp.int32, TILE, 0)
    lanes = lax.broadcasted_iota(jnp.int32, (96, 128), 1)
    tiles = [block[8 * i : 8 * i + 8, :] for i in range(16)]
    for s in range(4):
        mine = list(range(4 * s, 4 * s + 4))
        others = [i for i in range(16) if i not in mine]
        old = jnp.concatenate([tiles[i] for i in others], axis=0)
        for t in mine:
            cols = {i: [spread_tile(tiles[i][:, 8 * t + k : 8 * t + k + 1]) for k in range(8)] for i in mine}
            e = [[spread_tile(cols[t][j][k : k + 1, :]) if j <= k else None for j in range(8)] for k in range(8)]
            inside = (lane >= 8 * t) & (lane < 8 * t + 8)
            rows = [
                jnp.where(lane == 8 * t + k, 1.0, jnp.where(inside, 0.0, spread_tile(tiles[t][k : k + 1, :])))
                for k in range(8)
            ]
            new = solve8(e, rows)
            for i in mine:
                if i == t:
                    u = new[0]
                    for k in range(1, 8):
                        u = jnp.where(sub == k, new[k], u)
                else:
                    u = jnp.where(inside, 0.0, tiles[i])
                    p = [cols[i][k] * new[k] for k in range(8)]
                    u = u - (((p[0] + p[1]) + (p[2] + p[3])) + ((p[4] + p[5]) + (p[6] + p[7])))
                tiles[i] = u
        low, high = 32 * s, 32 * s + 32
        parts = [jnp.concatenate([tiles[i] for i in mine], axis=0)]
        if low:
            parts.insert(0, jnp.zeros((low, 128), F32))
        if high < 128:
            parts.append(jnp.zeros((128 - high, 128), F32))
        strip = jnp.concatenate(parts, axis=0)
        inside = (lanes >= low) & (lanes < high)
        fresh = jnp.where(inside, 0.0, old) - dot(jnp.where(inside, old, 0.0), strip, HIGHEST)
        for q, i in enumerate(others):
            tiles[i] = fresh[8 * q : 8 * q + 8]
    return jnp.concatenate(tiles, axis=0)


def linked(nbr_ref, patch, home):
    first = last = first_at = last_at = jnp.int32(0)
    for j in range(5):
        n = nbr_ref[j, patch]
        here = (n >> 3) == home
        last = jnp.where(here, n, last)
        last_at = jnp.where(here, j, last_at)
    for j in reversed(range(5)):
        n = nbr_ref[j, patch]
        here = (n >> 3) == home
        first = jnp.where(here, n, first)
        first_at = jnp.where(here, j, first_at)
    return first, first_at, last, last_at


def place():
    region, member = lax.axis_index("region"), lax.axis_index("member")
    regions = lax.axis_size("region")
    sides = (region, lax.rem(region + 1, regions), lax.rem(region + regions - 1, regions))
    return region, member, sides


def columns(member):
    return pl.ds(pl.multiple_of(member * 128, 128), 128)


def greet(peers):
    barrier = pltpu.get_barrier_semaphore()
    for peer in peers:
        pl.semaphore_signal(barrier, inc=1, device_id=peer, device_id_type=MESH)
    pl.semaphore_wait(barrier, len(peers))


def all_peers(member, sides):
    return [
        {"region": sides[s], "member": lax.rem(member + d, 8)}
        for d in range(8)
        for s in range(3)
        if (s, d) != (0, 0)
    ]


def remote(src, dst, send, recv, region, member):
    return pltpu.make_async_remote_copy(
        src_ref=src,
        dst_ref=dst,
        send_sem=send,
        recv_sem=recv,
        device_id={"region": region, "member": member},
        device_id_type=MESH,
    )


def row_copies(own, region, member, sides, nbr_ref, rows, sbuf, y_ref, send_sem, recv_sem):
    low = 0 if own else OBS
    sent = []
    for d in range(8):
        other = lax.rem(member + d, 8)
        for s in (1, 2, 0):
            first, _, last, _ = linked(nbr_ref, sides[s] * 8 + other, region)
            if s == 0:
                if own:
                    sbuf[s, d, 0:OBS, :] = rows[other]
                sbuf[s, d, OBS : 2 * OBS, :] = rows[first & 7]
            else:
                sbuf[s, d, 0:OBS, :] = rows[first & 7]
                sbuf[s, d, OBS : 2 * OBS, :] = rows[last & 7]
            start = low if s == 0 else 0
            if s == 0 and d == 0:
                y_ref[start : 2 * OBS, columns(member)] = sbuf[0, 0, start : 2 * OBS, :]
                continue
            copy = remote(
                sbuf.at[s, d, pl.ds(start, 2 * OBS - start)],
                y_ref.at[pl.ds(s * 128 + start, 2 * OBS - start), columns(member)],
                send_sem.at[s, d],
                recv_sem.at[s, member],
                sides[s],
                other,
            )
            copy.start()
            sent.append(copy)
    return sent


def await_rows(own, member, sides, sbuf, y_ref, send_sem, recv_sem):
    low = 0 if own else OBS
    for d in range(8):
        other = lax.rem(member + d, 8)
        for s in range(3):
            if (s, d) == (0, 0):
                continue
            start = low if s == 0 else 0
            remote(
                sbuf.at[s, d, pl.ds(start, 2 * OBS - start)],
                y_ref.at[pl.ds(s * 128 + start, 2 * OBS - start), columns(other)],
                send_sem.at[s, d],
                recv_sem.at[s, other],
                sides[s],
                other,
            ).wait_recv()


def scatter_kernel(state_ref, cell_ref, nbr_ref, y_ref, x_ref, rows, sbuf, xbuf, send_sem, recv_sem, xsend_sem, xrecv_sem):
    region, member, sides = place()
    greet(all_peers(member, sides))
    lane = lax.broadcasted_iota(jnp.int32, (OBS, 256), 1)
    for q in range(8):
        cell = jnp.sum(jnp.where(lane == region * 8 + q, cell_ref[0], 0), axis=1, keepdims=True)
        picked = jnp.where(lane == cell, 1.0, 0.0)
        rows[q] = dot_t(picked, state_ref[:, q, :], HIGHEST)
    sent = row_copies(True, region, member, sides, nbr_ref, rows, sbuf, y_ref, send_sem, recv_sem)
    for q in range(8):
        xbuf[q] = state_ref[:, q, :].T
    for d in range(1, 8):
        other = lax.rem(member + d, 8)
        copy = remote(xbuf.at[other], x_ref.at[:, columns(member)], xsend_sem.at[d], xrecv_sem.at[member], region, other)
        copy.start()
        sent.append(copy)
    x_ref[:, columns(member)] = xbuf[member]
    await_rows(True, member, sides, sbuf, y_ref, send_sem, recv_sem)
    for d in range(1, 8):
        other = lax.rem(member + d, 8)
        remote(xbuf.at[other], x_ref.at[:, columns(other)], xsend_sem.at[d], xrecv_sem.at[other], region, other).wait_recv()
    for copy in sent:
        copy.wait_send()


def rows_kernel(own_ref, nbr_ref, y_ref, rows, sbuf, send_sem, recv_sem, asend_sem, arecv_sem):
    region, member, sides = place()
    greet(all_peers(member, sides))
    first = []
    for d in range(1, 8):
        other = lax.rem(member + d, 8)
        copy = remote(own_ref.at[:, columns(other)], rows.at[member], asend_sem.at[d], arecv_sem.at[member], region, other)
        copy.start()
        first.append(copy)
    rows[member] = own_ref[:, columns(member)]
    y_ref[0:OBS, :] = own_ref[...]
    for d in range(1, 8):
        other = lax.rem(member + d, 8)
        remote(own_ref.at[:, columns(other)], rows.at[other], asend_sem.at[d], arecv_sem.at[other], region, other).wait_recv()
    sent = row_copies(False, region, member, sides, nbr_ref, rows, sbuf, y_ref, send_sem, recv_sem)
    await_rows(False, member, sides, sbuf, y_ref, send_sem, recv_sem)
    for copy in first + sent:
        copy.wait_send()


def return_kernel(x_ref, o_ref, tbuf, send_sem, recv_sem):
    region, member, sides = place()
    greet([{"region": region, "member": lax.rem(member + d, 8)} for d in range(1, 8)])
    sent = []
    for d in range(1, 8):
        other = lax.rem(member + d, 8)
        tbuf[d] = x_ref[:, columns(other)].T
        copy = remote(tbuf.at[d], o_ref.at[member], send_sem.at[d], recv_sem.at[member], region, other)
        copy.start()
        sent.append(copy)
    o_ref[member] = x_ref[:, columns(member)].T
    for d in range(1, 8):
        other = lax.rem(member + d, 8)
        remote(tbuf.at[d], o_ref.at[other], send_sem.at[d], recv_sem.at[other], region, other).wait_recv()
    for copy in sent:
        copy.wait_send()


def analysis_kernel(batch, more, y_ref, x_ref, val_ref, var_ref, cell_ref, nbr_ref, *rest):
    if more:
        xo_ref, r_ref, yh, yl, ah, al, cov, inno, var, cross = rest
    else:
        xo_ref, yh, yl, ah, al, cov, inno, var, cross = rest
    region, member, sides = place()
    patch = region * 8 + member
    lane = lax.broadcasted_iota(jnp.int32, (OBS, 256), 1)
    same, same_at, _, _ = linked(nbr_ref, patch, region)
    slots = [(patch, jnp.int32(-1)), (same, same_at)]
    for side in (sides[2], sides[1]):
        f, fa, l, la = linked(nbr_ref, patch, side)
        slots += [(f, fa), (l, la)]
    for i, (n, at) in enumerate(slots):
        here = lane == n
        value = jnp.sum(jnp.where(here, val_ref[batch], 0.0), axis=1, keepdims=True)
        noise = jnp.sum(jnp.where(here, var_ref[batch], 0.0), axis=1, keepdims=True)
        widening = (at + 2).astype(F32)
        inno[i * OBS : (i + 1) * OBS, :] = jnp.broadcast_to(value, (OBS, 128))
        var[i * OBS : (i + 1) * OBS, :] = jnp.broadcast_to(noise * widening, (OBS, 128))

    def centre(i, _):
        at = pl.ds(pl.multiple_of(i * 32, 32), 32)
        y = y_ref[at, :]
        mean = jnp.sum(y, axis=1, keepdims=True) * (1.0 / 1024.0)
        yh[at, :], yl[at, :] = split(y - mean)
        inno[at, :] = inno[at, :] - mean
        return 0

    lax.fori_loop(0, 12, centre, 0)

    def covariance(i, _):
        at = pl.ds(pl.multiple_of(i * 128, 128), 128)
        high, low = yh[at, :], yl[at, :]
        total = dot_t(high, yh[...]) + (dot_t(high, yl[...]) + dot_t(low, yh[...]))
        row = lax.broadcasted_iota(jnp.int32, (128, 384), 0) + i * 128
        col = lax.broadcasted_iota(jnp.int32, (128, 384), 1)
        wide = jnp.concatenate([var[at, :]] * 3, axis=1)
        cov[at, :] = total * (1.0 / 1023.0) + jnp.where(row == col, wide, 0.0)
        return 0

    lax.fori_loop(0, 3, covariance, 0)

    def eliminate(k, _):
        at = pl.ds(pl.multiple_of(k * 128, 128), 128)
        inv = inverse128(cov[at, at])
        row = lax.broadcasted_iota(jnp.int32, (128, 384), 0) + k * 128
        col = lax.broadcasted_iota(jnp.int32, (128, 384), 1)
        inside = (col >= k * 128) & (col < k * 128 + 128)
        top = dot(inv, jnp.where(inside, jnp.where(row == col, 1.0, 0.0), cov[at, :]), HIGHEST)
        for i in range(3):
            part = slice(i * 128, i * 128 + 128)
            cov[part, :] = jnp.where(inside, 0.0, cov[part, :]) - dot(cov[part, at], top, HIGHEST)
        cov[at, :] = top
        return 0

    lax.fori_loop(0, 3, eliminate, 0)

    def anomaly(i, _):
        at = pl.ds(pl.multiple_of(i * 32, 32), 32)
        x = x_ref[at, :]
        ah[at, :], al[at, :] = split(x - jnp.sum(x, axis=1, keepdims=True) * (1.0 / 1024.0))
        return 0

    lax.fori_loop(0, 8, anomaly, 0)
    high, low = ah[...], al[...]
    cross[...] = (dot_t(high, yh[...]) + (dot_t(high, yl[...]) + dot_t(low, yh[...]))) * (1.0 / 1023.0)
    gain = dot(cross[...], cov[...], HIGHEST)
    shift = dot(gain, inno[...], HIGHEST)
    gh, gl = split(-0.5 * gain)
    if more:
        here = lane == patch
        cell = jnp.sum(jnp.where(here, cell_ref[batch + 1], 0), axis=1, keepdims=True)
        picked = jnp.where(lane == cell, 1.0, 0.0)
    for i in range(8):
        at = slice(i * 128, i * 128 + 128)
        h, l = yh[:, at], yl[:, at]
        x = x_ref[:, at] + (shift + (dot(gh, h) + (dot(gh, l) + dot(gl, h))))
        xo_ref[:, at] = x
        if more:
            r_ref[:, at] = dot(picked, x, HIGHEST)


def analysis(batch, more, y, x, values, variances, cells, nbr):
    out = [jax.ShapeDtypeStruct((256, 1024), F32)]
    if more:
        out.append(jax.ShapeDtypeStruct((OBS, 1024), F32))
    return pl.pallas_call(
        functools.partial(analysis_kernel, batch, more),
        out_shape=out,
        in_specs=[VMEM] * 5 + [SMEM],
        out_specs=[VMEM] * len(out),
        scratch_shapes=[
            pltpu.VMEM((384, 1024), BF16),
            pltpu.VMEM((384, 1024), BF16),
            pltpu.VMEM((256, 1024), BF16),
            pltpu.VMEM((256, 1024), BF16),
            pltpu.VMEM((384, 384), F32),
            pltpu.VMEM((384, 128), F32),
            pltpu.VMEM((384, 128), F32),
            pltpu.VMEM((256, 384), F32),
        ],
        compiler_params=pltpu.CompilerParams(vmem_limit_bytes=48 * 1024 * 1024),
        name="analysis",
    )(y, x, values, variances, cells, nbr)


DMA = pltpu.SemaphoreType.DMA


def params(number):
    return pltpu.CompilerParams(collective_id=number, has_side_effects=True, vmem_limit_bytes=48 * 1024 * 1024)


def on_device(state, neighbours, obs_cell, obs_values, obs_var):
    nbr = jnp.transpose(neighbours, (1, 0))
    cells = jnp.transpose(obs_cell, (1, 2, 0))
    values = jnp.transpose(obs_values, (1, 2, 0))
    variances = jnp.transpose(obs_var, (1, 2, 0))
    y, x = pl.pallas_call(
        scatter_kernel,
        out_shape=[jax.ShapeDtypeStruct((384, 1024), F32), jax.ShapeDtypeStruct((256, 1024), F32)],
        in_specs=[VMEM, VMEM, SMEM],
        out_specs=[VMEM, VMEM],
        scratch_shapes=[
            pltpu.VMEM((8, OBS, 128), F32),
            pltpu.VMEM((3, 8, 128, 128), F32),
            pltpu.VMEM((8, 256, 128), F32),
            DMA((3, 8)),
            DMA((3, 8)),
            DMA((8,)),
            DMA((8,)),
        ],
        compiler_params=params(0),
        name="scatter",
    )(state, cells, nbr)
    x, own = analysis(0, True, y, x, values, variances, cells, nbr)
    (y,) = pl.pallas_call(
        rows_kernel,
        out_shape=[jax.ShapeDtypeStruct((384, 1024), F32)],
        in_specs=[VMEM, SMEM],
        out_specs=[VMEM],
        scratch_shapes=[
            pltpu.VMEM((8, OBS, 128), F32),
            pltpu.VMEM((3, 8, 128, 128), F32),
            DMA((3, 8)),
            DMA((3, 8)),
            DMA((8,)),
            DMA((8,)),
        ],
        compiler_params=params(1),
        name="rows",
    )(own, nbr)
    (x,) = analysis(1, False, y, x, values, variances, cells, nbr)
    (out,) = pl.pallas_call(
        return_kernel,
        out_shape=[jax.ShapeDtypeStruct((8, 128, 256), F32)],
        in_specs=[VMEM],
        out_specs=[VMEM],
        scratch_shapes=[pltpu.VMEM((8, 128, 256), F32), DMA((8,)), DMA((8,))],
        compiler_params=params(2),
        name="give_back",
    )(x)
    return jnp.transpose(out, (1, 0, 2))


def solution(mesh):
    in_specs = (P("member", "region", None), P(), P(), P(), P())
    out_specs = P("member", "region", None)
    return jax.shard_map(on_device, mesh=mesh, in_specs=in_specs, out_specs=out_specs, check_vma=False)
```

```python
import jax
import jax.numpy as jnp
from jax import lax
from jax.experimental import pallas as pl
from jax.experimental.pallas import tpu as pltpu
from jax.sharding import PartitionSpec as P

F32 = jnp.float32
BF16 = jnp.bfloat16
HIGHEST = lax.Precision.HIGHEST
MESH = pl.DeviceIdType.MESH
TILE = (8, 128)
OBS = 64
VMEM = pl.BlockSpec(memory_space=pltpu.VMEM)
SMEM = pl.BlockSpec(memory_space=pltpu.SMEM)
ANY = pl.BlockSpec(memory_space=pl.ANY)
DMA = pltpu.SemaphoreType.DMA


def dot(a, b, precision=None):
    return lax.dot_general(a, b, (((1,), (0,)), ((), ())), precision=precision, preferred_element_type=F32)


def dot_t(a, b, precision=None):
    return lax.dot_general(a, b, (((1,), (1,)), ((), ())), precision=precision, preferred_element_type=F32)


def split(x):
    high = x.astype(BF16)
    return high, (x - high.astype(F32)).astype(BF16)


def spread_tile(x):
    return jnp.broadcast_to(x, TILE)


def solve8(e, r):
    m = {}
    q = [None] * 8
    for i in range(0, 8, 2):
        a, b, d = e[i][i], e[i + 1][i], e[i + 1][i + 1]
        inv = 1.0 / (a * d - b * b)
        ai, bi, di = d * inv, b * inv, a * inv
        for k in range(i + 2, 8):
            m[k, i] = e[k][i] * ai - e[k][i + 1] * bi
            m[k, i + 1] = e[k][i + 1] * di - e[k][i] * bi
        for k in range(i + 2, 8):
            for j in range(i + 2, k + 1):
                e[k][j] = e[k][j] - (m[k, i] * e[j][i] + m[k, i + 1] * e[j][i + 1])
        for k in range(i + 2, 8):
            r[k] = r[k] - (m[k, i] * r[i] + m[k, i + 1] * r[i + 1])
        q[i], q[i + 1] = ai * r[i] - bi * r[i + 1], di * r[i + 1] - bi * r[i]
    for i in range(6, 0, -2):
        for k in range(i):
            q[k] = q[k] - (m[i, k] * q[i] + m[i + 1, k] * q[i + 1])
    return q


def inverse128(block):
    lane = lax.broadcasted_iota(jnp.int32, TILE, 1)
    sub = lax.broadcasted_iota(jnp.int32, TILE, 0)
    lanes = lax.broadcasted_iota(jnp.int32, (96, 128), 1)
    tiles = [block[8 * i : 8 * i + 8, :] for i in range(16)]
    for s in range(4):
        mine = list(range(4 * s, 4 * s + 4))
        others = [i for i in range(16) if i not in mine]
        old = jnp.concatenate([tiles[i] for i in others], axis=0)
        for t in mine:
            cols = {i: [spread_tile(tiles[i][:, 8 * t + k : 8 * t + k + 1]) for k in range(8)] for i in mine}
            e = [[spread_tile(cols[t][j][k : k + 1, :]) if j <= k else None for j in range(8)] for k in range(8)]
            inside = (lane >= 8 * t) & (lane < 8 * t + 8)
            rows = [
                jnp.where(lane == 8 * t + k, 1.0, jnp.where(inside, 0.0, spread_tile(tiles[t][k : k + 1, :])))
                for k in range(8)
            ]
            new = solve8(e, rows)
            for i in mine:
                if i == t:
                    u = new[0]
                    for k in range(1, 8):
                        u = jnp.where(sub == k, new[k], u)
                else:
                    u = jnp.where(inside, 0.0, tiles[i])
                    p = [cols[i][k] * new[k] for k in range(8)]
                    u = u - (((p[0] + p[1]) + (p[2] + p[3])) + ((p[4] + p[5]) + (p[6] + p[7])))
                tiles[i] = u
        low, high = 32 * s, 32 * s + 32
        parts = [jnp.concatenate([tiles[i] for i in mine], axis=0)]
        if low:
            parts.insert(0, jnp.zeros((low, 128), F32))
        if high < 128:
            parts.append(jnp.zeros((128 - high, 128), F32))
        strip = jnp.concatenate(parts, axis=0)
        inside = (lanes >= low) & (lanes < high)
        fresh = jnp.where(inside, 0.0, old) - dot(jnp.where(inside, old, 0.0), strip, HIGHEST)
        for q, i in enumerate(others):
            tiles[i] = fresh[8 * q : 8 * q + 8]
    return jnp.concatenate(tiles, axis=0)


def linked(nbr_ref, patch, home):
    first = last = first_at = last_at = jnp.int32(0)
    for j in range(5):
        n = nbr_ref[j, patch]
        here = (n >> 3) == home
        last = jnp.where(here, n, last)
        last_at = jnp.where(here, j, last_at)
    for j in reversed(range(5)):
        n = nbr_ref[j, patch]
        here = (n >> 3) == home
        first = jnp.where(here, n, first)
        first_at = jnp.where(here, j, first_at)
    return first, first_at, last, last_at


def place():
    region, member = lax.axis_index("region"), lax.axis_index("member")
    regions = lax.axis_size("region")
    sides = (region, lax.rem(region + 1, regions), lax.rem(region + regions - 1, regions))
    return region, member, sides


def columns(member):
    return pl.ds(pl.multiple_of(member * 128, 128), 128)


def all_peers(member, sides):
    return [
        {"region": sides[s], "member": lax.rem(member + d, 8)}
        for d in range(8)
        for s in range(3)
        if (s, d) != (0, 0)
    ]


def remote(src, dst, send, recv, region, member):
    return pltpu.make_async_remote_copy(
        src_ref=src,
        dst_ref=dst,
        send_sem=send,
        recv_sem=recv,
        device_id={"region": region, "member": member},
        device_id_type=MESH,
    )


def exchange(batch, region, member, sides, nbr_ref, rows, sbuf, y_ref, send_sem, recv_sem):
    low = OBS if batch else 0
    sent = []
    for d in range(8):
        other = lax.rem(member + d, 8)
        for s in (1, 2, 0):
            first, _, last, _ = linked(nbr_ref, sides[s] * 8 + other, region)
            if s == 0:
                if batch == 0:
                    sbuf[batch, s, d, 0:OBS, :] = rows[batch, other]
                sbuf[batch, s, d, OBS : 2 * OBS, :] = rows[batch, first & 7]
            else:
                sbuf[batch, s, d, 0:OBS, :] = rows[batch, first & 7]
                sbuf[batch, s, d, OBS : 2 * OBS, :] = rows[batch, last & 7]
            start = low if s == 0 else 0
            if s == 0 and d == 0:
                y_ref[batch, start : 2 * OBS, columns(member)] = sbuf[batch, 0, 0, start : 2 * OBS, :]
                continue
            copy = remote(
                sbuf.at[batch, s, d, pl.ds(start, 2 * OBS - start)],
                y_ref.at[batch, pl.ds(s * 128 + start, 2 * OBS - start), columns(member)],
                send_sem.at[batch, s, d],
                recv_sem.at[batch, s, member],
                sides[s],
                other,
            )
            copy.start()
            sent.append(copy)
    return sent


def await_rows(batch, member, sides, sbuf, y_ref, send_sem, recv_sem):
    low = OBS if batch else 0
    for d in range(8):
        other = lax.rem(member + d, 8)
        for s in range(3):
            if (s, d) == (0, 0):
                continue
            start = low if s == 0 else 0
            remote(
                sbuf.at[batch, s, d, pl.ds(start, 2 * OBS - start)],
                y_ref.at[batch, pl.ds(s * 128 + start, 2 * OBS - start), columns(other)],
                send_sem.at[batch, s, d],
                recv_sem.at[batch, s, other],
                sides[s],
                other,
            ).wait_recv()


def observed(batch, patch, region, sides, nbr_ref, val_ref, var_ref, inno, var):
    lane = lax.broadcasted_iota(jnp.int32, (OBS, 256), 1)
    same, same_at, _, _ = linked(nbr_ref, patch, region)
    slots = [(patch, jnp.int32(-1)), (same, same_at)]
    for side in (sides[2], sides[1]):
        f, fa, l, la = linked(nbr_ref, patch, side)
        slots += [(f, fa), (l, la)]
    for i, (n, at) in enumerate(slots):
        here = lane == n
        value = jnp.sum(jnp.where(here, val_ref[batch], 0.0), axis=1, keepdims=True)
        noise = jnp.sum(jnp.where(here, var_ref[batch], 0.0), axis=1, keepdims=True)
        widening = (at + 2).astype(F32)
        inno[i * OBS : (i + 1) * OBS, :] = jnp.broadcast_to(value, (OBS, 128))
        var[i * OBS : (i + 1) * OBS, :] = jnp.broadcast_to(noise * widening, (OBS, 128))


def inverse_covariance(batch, y_ref, yh, yl, cov, inno, var):
    def centre(i, _):
        at = pl.ds(pl.multiple_of(i * 32, 32), 32)
        y = y_ref[batch, at, :]
        mean = jnp.sum(y, axis=1, keepdims=True) * (1.0 / 1024.0)
        yh[at, :], yl[at, :] = split(y - mean)
        inno[at, :] = inno[at, :] - mean
        return 0

    lax.fori_loop(0, 12, centre, 0)

    def covariance(i, _):
        at = pl.ds(pl.multiple_of(i * 128, 128), 128)
        high, low = yh[at, :], yl[at, :]
        total = dot_t(high, yh[...]) + (dot_t(high, yl[...]) + dot_t(low, yh[...]))
        row = lax.broadcasted_iota(jnp.int32, (128, 384), 0) + i * 128
        col = lax.broadcasted_iota(jnp.int32, (128, 384), 1)
        wide = jnp.concatenate([var[at, :]] * 3, axis=1)
        cov[at, :] = total * (1.0 / 1023.0) + jnp.where(row == col, wide, 0.0)
        return 0

    lax.fori_loop(0, 3, covariance, 0)

    def eliminate(k, _):
        at = pl.ds(pl.multiple_of(k * 128, 128), 128)
        inv = inverse128(cov[at, at])
        row = lax.broadcasted_iota(jnp.int32, (128, 384), 0) + k * 128
        col = lax.broadcasted_iota(jnp.int32, (128, 384), 1)
        inside = (col >= k * 128) & (col < k * 128 + 128)
        top = dot(inv, jnp.where(inside, jnp.where(row == col, 1.0, 0.0), cov[at, :]), HIGHEST)
        for i in range(3):
            part = slice(i * 128, i * 128 + 128)
            cov[part, :] = jnp.where(inside, 0.0, cov[part, :]) - dot(cov[part, at], top, HIGHEST)
        cov[at, :] = top
        return 0

    lax.fori_loop(0, 3, eliminate, 0)


def gain_of(x_ref, yh, yl, ah, al, cov, inno):
    def anomaly(i, _):
        at = pl.ds(pl.multiple_of(i * 32, 32), 32)
        x = x_ref[at, :]
        ah[at, :], al[at, :] = split(x - jnp.sum(x, axis=1, keepdims=True) * (1.0 / 1024.0))
        return 0

    lax.fori_loop(0, 8, anomaly, 0)
    high, low = ah[...], al[...]
    cross = (dot_t(high, yh[...]) + (dot_t(high, yl[...]) + dot_t(low, yh[...]))) * (1.0 / 1023.0)
    gain = dot(cross, cov[...], HIGHEST)
    return gain, dot(gain, inno[...], HIGHEST)


def whole_kernel(
    state_hbm, cell_hbm, val_hbm, var_hbm, nbr_ref, o_ref,
    state_ref, cell_ref, val_ref, var_ref,
    rows, sbuf, y_ref, xbuf, x_ref, x2_ref, rbuf, tbuf,
    yh, yl, ah, al, cov, inno, var,
    load_sem, send_sem, recv_sem, xsend_sem, xrecv_sem, asend_sem, arecv_sem, osend_sem, orecv_sem,
):
    region, member, sides = place()
    patch = region * 8 + member
    lane = lax.broadcasted_iota(jnp.int32, (OBS, 256), 1)
    loads = [
        pltpu.make_async_copy(src, dst, load_sem.at[i])
        for i, (src, dst) in enumerate(
            ((state_hbm, state_ref), (cell_hbm, cell_ref), (val_hbm, val_ref), (var_hbm, var_ref))
        )
    ]
    for load in loads:
        load.start()
    peers = all_peers(member, sides)
    barrier = pltpu.get_barrier_semaphore()
    for peer in peers:
        pl.semaphore_signal(barrier, inc=1, device_id=peer, device_id_type=MESH)
    loads[0].wait()
    loads[1].wait()
    for q in range(8):
        cell = jnp.sum(jnp.where(lane == region * 8 + q, cell_ref[0], 0), axis=1, keepdims=True)
        picked = jnp.where(lane == cell, 1.0, 0.0)
        rows[0, q] = dot_t(picked, state_ref[:, q, :], HIGHEST)
    pl.semaphore_wait(barrier, len(peers))

    sent = exchange(0, region, member, sides, nbr_ref, rows, sbuf, y_ref, send_sem, recv_sem)
    for q in range(8):
        xbuf[q] = state_ref[:, q, :].T
    x_ref[:, columns(member)] = xbuf[member]
    loads[2].wait()
    loads[3].wait()
    observed(0, patch, region, sides, nbr_ref, val_ref, var_ref, inno, var)
    await_rows(0, member, sides, sbuf, y_ref, send_sem, recv_sem)
    for d in range(1, 8):
        other = lax.rem(member + d, 8)
        copy = remote(xbuf.at[other], x_ref.at[:, columns(member)], xsend_sem.at[d], xrecv_sem.at[member], region, other)
        copy.start()
        sent.append(copy)
    inverse_covariance(0, y_ref, yh, yl, cov, inno, var)
    for d in range(1, 8):
        other = lax.rem(member + d, 8)
        remote(xbuf.at[other], x_ref.at[:, columns(other)], xsend_sem.at[d], xrecv_sem.at[other], region, other).wait_recv()

    gain, shift = gain_of(x_ref, yh, yl, ah, al, cov, inno)
    cell = jnp.sum(jnp.where(lane == patch, cell_ref[1], 0), axis=1, keepdims=True)
    picked = jnp.where(lane == cell, 1.0, 0.0)
    pshift = dot(picked, shift, HIGHEST)
    ph, pl_ = split(dot(picked, -0.5 * gain, HIGHEST))
    for d in range(8):
        other = lax.rem(member + d, 8)
        at = columns(other)
        h, l = yh[:, at], yl[:, at]
        r = dot(picked, x_ref[:, at], HIGHEST) + (pshift + (dot(ph, h) + (dot(ph, l) + dot(pl_, h))))
        rbuf[d] = r
        y_ref[1, 0:OBS, at] = r
        if d == 0:
            rows[1, member] = r
            continue
        copy = remote(rbuf.at[d], rows.at[1, member], asend_sem.at[d], arecv_sem.at[member], region, other)
        copy.start()
        sent.append(copy)
    gh, gl = split(-0.5 * gain)
    for i in range(8):
        at = slice(i * 128, i * 128 + 128)
        h, l = yh[:, at], yl[:, at]
        x2_ref[:, at] = x_ref[:, at] + (shift + (dot(gh, h) + (dot(gh, l) + dot(gl, h))))
    for d in range(1, 8):
        other = lax.rem(member + d, 8)
        remote(rbuf.at[d], rows.at[1, other], asend_sem.at[d], arecv_sem.at[other], region, other).wait_recv()

    sent += exchange(1, region, member, sides, nbr_ref, rows, sbuf, y_ref, send_sem, recv_sem)
    observed(1, patch, region, sides, nbr_ref, val_ref, var_ref, inno, var)
    await_rows(1, member, sides, sbuf, y_ref, send_sem, recv_sem)
    inverse_covariance(1, y_ref, yh, yl, cov, inno, var)
    gain, shift = gain_of(x2_ref, yh, yl, ah, al, cov, inno)
    gh, gl = split(-0.5 * gain)
    for d in (1, 2, 3, 4, 5, 6, 7, 0):
        other = lax.rem(member + d, 8)
        at = columns(other)
        h, l = yh[:, at], yl[:, at]
        x = x2_ref[:, at] + (shift + (dot(gh, h) + (dot(gh, l) + dot(gl, h))))
        if d == 0:
            o_ref[member] = x.T
            continue
        tbuf[d] = x.T
        copy = remote(tbuf.at[d], o_ref.at[member], osend_sem.at[d], orecv_sem.at[member], region, other)
        copy.start()
        sent.append(copy)
    for d in range(1, 8):
        other = lax.rem(member + d, 8)
        remote(tbuf.at[d], o_ref.at[other], osend_sem.at[d], orecv_sem.at[other], region, other).wait_recv()
    for copy in sent:
        copy.wait_send()


def on_device(state, neighbours, obs_cell, obs_values, obs_var):
    small = pltpu.VMEM((2, OBS, 256), F32)
    out = pl.pallas_call(
        whole_kernel,
        out_shape=jax.ShapeDtypeStruct((8, 128, 256), F32),
        in_specs=[ANY] * 4 + [SMEM],
        out_specs=VMEM,
        scratch_shapes=[
            pltpu.VMEM((128, 8, 256), F32),
            pltpu.VMEM((2, OBS, 256), jnp.int32),
            small,
            small,
            pltpu.VMEM((2, 8, OBS, 128), F32),
            pltpu.VMEM((2, 3, 8, 128, 128), F32),
            pltpu.VMEM((2, 384, 1024), F32),
            pltpu.VMEM((8, 256, 128), F32),
            pltpu.VMEM((256, 1024), F32),
            pltpu.VMEM((256, 1024), F32),
            pltpu.VMEM((8, OBS, 128), F32),
            pltpu.VMEM((8, 128, 256), F32),
            pltpu.VMEM((384, 1024), BF16),
            pltpu.VMEM((384, 1024), BF16),
            pltpu.VMEM((256, 1024), BF16),
            pltpu.VMEM((256, 1024), BF16),
            pltpu.VMEM((384, 384), F32),
            pltpu.VMEM((384, 128), F32),
            pltpu.VMEM((384, 128), F32),
            DMA((4,)),
            DMA((2, 3, 8)),
            DMA((2, 3, 8)),
            DMA((8,)),
            DMA((8,)),
            DMA((8,)),
            DMA((8,)),
            DMA((8,)),
            DMA((8,)),
        ],
        compiler_params=pltpu.CompilerParams(
            collective_id=0, has_side_effects=True, vmem_limit_bytes=60 * 1024 * 1024
        ),
        name="whole",
    )(
        state,
        jnp.transpose(obs_cell, (1, 2, 0)),
        jnp.transpose(obs_values, (1, 2, 0)),
        jnp.transpose(obs_var, (1, 2, 0)),
        jnp.transpose(neighbours, (1, 0)),
    )
    return jnp.transpose(out, (1, 0, 2))


def solution(mesh):
    in_specs = (P("member", "region", None), P(), P(), P(), P())
    out_specs = P("member", "region", None)
    return jax.shard_map(on_device, mesh=mesh, in_specs=in_specs, out_specs=out_specs, check_vma=False)
```

```python
import jax
import jax.numpy as jnp
from jax import lax
from jax.experimental import pallas as pl
from jax.experimental.pallas import tpu as pltpu
from jax.sharding import PartitionSpec as P

F32 = jnp.float32
BF16 = jnp.bfloat16
HIGHEST = lax.Precision.HIGHEST
MESH = pl.DeviceIdType.MESH
TILE = (8, 128)
OBS = 64
VMEM = pl.BlockSpec(memory_space=pltpu.VMEM)
SMEM = pl.BlockSpec(memory_space=pltpu.SMEM)
ANY = pl.BlockSpec(memory_space=pl.ANY)
DMA = pltpu.SemaphoreType.DMA


def dot(a, b, precision=None):
    return lax.dot_general(a, b, (((1,), (0,)), ((), ())), precision=precision, preferred_element_type=F32)


def dot_t(a, b, precision=None):
    return lax.dot_general(a, b, (((1,), (1,)), ((), ())), precision=precision, preferred_element_type=F32)


def split(x):
    high = x.astype(BF16)
    return high, (x - high.astype(F32)).astype(BF16)


def spread_tile(x):
    return jnp.broadcast_to(x, TILE)


def solve8(e, r):
    m = {}
    q = [None] * 8
    for i in range(0, 8, 2):
        a, b, d = e[i][i], e[i + 1][i], e[i + 1][i + 1]
        inv = 1.0 / (a * d - b * b)
        ai, bi, di = d * inv, b * inv, a * inv
        for k in range(i + 2, 8):
            m[k, i] = e[k][i] * ai - e[k][i + 1] * bi
            m[k, i + 1] = e[k][i + 1] * di - e[k][i] * bi
        for k in range(i + 2, 8):
            for j in range(i + 2, k + 1):
                e[k][j] = e[k][j] - (m[k, i] * e[j][i] + m[k, i + 1] * e[j][i + 1])
        for k in range(i + 2, 8):
            r[k] = r[k] - (m[k, i] * r[i] + m[k, i + 1] * r[i + 1])
        q[i], q[i + 1] = ai * r[i] - bi * r[i + 1], di * r[i + 1] - bi * r[i]
    for i in range(6, 0, -2):
        for k in range(i):
            q[k] = q[k] - (m[i, k] * q[i] + m[i + 1, k] * q[i + 1])
    return q


def inverse128(block):
    lane = lax.broadcasted_iota(jnp.int32, TILE, 1)
    sub = lax.broadcasted_iota(jnp.int32, TILE, 0)
    front = lax.broadcasted_iota(jnp.int32, (96, 128), 1) < 32

    def strip(_, matrix):
        tiles = [matrix[8 * i : 8 * i + 8, :] for i in range(4)]
        old = matrix[32:, :]
        for t in range(4):
            cols = [[spread_tile(tile[:, 8 * t + k : 8 * t + k + 1]) for k in range(8)] for tile in tiles]
            e = [[spread_tile(cols[t][j][k : k + 1, :]) if j <= k else None for j in range(8)] for k in range(8)]
            inside = (lane >= 8 * t) & (lane < 8 * t + 8)
            rows = [
                jnp.where(lane == 8 * t + k, 1.0, jnp.where(inside, 0.0, spread_tile(tiles[t][k : k + 1, :])))
                for k in range(8)
            ]
            new = solve8(e, rows)
            for i in range(4):
                if i == t:
                    u = new[0]
                    for k in range(1, 8):
                        u = jnp.where(sub == k, new[k], u)
                else:
                    p = [cols[i][k] * new[k] for k in range(8)]
                    u = jnp.where(inside, 0.0, tiles[i])
                    u = u - (((p[0] + p[1]) + (p[2] + p[3])) + ((p[4] + p[5]) + (p[6] + p[7])))
                tiles[i] = u
        top = jnp.concatenate(tiles, axis=0)
        padded = jnp.concatenate([top, jnp.zeros((96, 128), F32)], axis=0)
        fresh = jnp.where(front, 0.0, old) - dot(jnp.where(front, old, 0.0), padded, HIGHEST)
        return pltpu.roll(jnp.concatenate([fresh, top], axis=0), 96, 1)

    return lax.fori_loop(0, 4, strip, block)


def linked(nbr_ref, patch, home):
    first = last = first_at = last_at = jnp.int32(0)
    for j in range(5):
        n = nbr_ref[j, patch]
        here = (n >> 3) == home
        last = jnp.where(here, n, last)
        last_at = jnp.where(here, j, last_at)
    for j in reversed(range(5)):
        n = nbr_ref[j, patch]
        here = (n >> 3) == home
        first = jnp.where(here, n, first)
        first_at = jnp.where(here, j, first_at)
    return first, first_at, last, last_at


def place():
    region, member = lax.axis_index("region"), lax.axis_index("member")
    regions = lax.axis_size("region")
    sides = (region, lax.rem(region + 1, regions), lax.rem(region + regions - 1, regions))
    return region, member, sides


def columns(member):
    return pl.ds(pl.multiple_of(member * 128, 128), 128)


def all_peers(member, sides):
    return [
        {"region": sides[s], "member": lax.rem(member + d, 8)}
        for d in range(8)
        for s in range(3)
        if (s, d) != (0, 0)
    ]


def remote(src, dst, send, recv, region, member):
    return pltpu.make_async_remote_copy(
        src_ref=src,
        dst_ref=dst,
        send_sem=send,
        recv_sem=recv,
        device_id={"region": region, "member": member},
        device_id_type=MESH,
    )


def start_of(batch, s):
    return OBS if batch and s == 0 else 0


def exchange(batch, region, member, sides, nbr_ref, rows, sbuf, y_ref, send_sem, recv_sem):
    sent = []
    for s in range(3):
        start = start_of(batch, s)
        for d in range(8):
            other = lax.rem(member + d, 8)
            first, _, last, _ = linked(nbr_ref, sides[s] * 8 + other, region)
            if s == 0:
                if batch == 0:
                    sbuf[batch, s, d, 0:OBS, :] = rows[batch, other]
                sbuf[batch, s, d, OBS : 2 * OBS, :] = rows[batch, first & 7]
            else:
                sbuf[batch, s, d, 0:OBS, :] = rows[batch, first & 7]
                sbuf[batch, s, d, OBS : 2 * OBS, :] = rows[batch, last & 7]
            if s == 0 and d == 0:
                y_ref[batch, start : 2 * OBS, columns(member)] = sbuf[batch, 0, 0, start : 2 * OBS, :]
                continue
            copy = remote(
                sbuf.at[batch, s, d, pl.ds(start, 2 * OBS - start)],
                y_ref.at[batch, pl.ds(s * 128 + start, 2 * OBS - start), columns(member)],
                send_sem.at[batch, s, d],
                recv_sem.at[batch, s, member],
                sides[s],
                other,
            )
            copy.start()
            sent.append(copy)
    return sent


def await_side(batch, s, member, sides, sbuf, y_ref, send_sem, recv_sem):
    start = start_of(batch, s)
    for d in range(8):
        if (s, d) == (0, 0):
            continue
        other = lax.rem(member + d, 8)
        remote(
            sbuf.at[batch, s, d, pl.ds(start, 2 * OBS - start)],
            y_ref.at[batch, pl.ds(s * 128 + start, 2 * OBS - start), columns(other)],
            send_sem.at[batch, s, d],
            recv_sem.at[batch, s, other],
            sides[s],
            other,
        ).wait_recv()


def observed(batch, patch, region, sides, nbr_ref, val_ref, var_ref, inno, var):
    lane = lax.broadcasted_iota(jnp.int32, (OBS, 256), 1)
    same, same_at, _, _ = linked(nbr_ref, patch, region)
    slots = [(patch, jnp.int32(-1)), (same, same_at)]
    for side in (sides[2], sides[1]):
        f, fa, l, la = linked(nbr_ref, patch, side)
        slots += [(f, fa), (l, la)]
    for i, (n, at) in enumerate(slots):
        here = lane == n
        value = jnp.sum(jnp.where(here, val_ref[batch], 0.0), axis=1, keepdims=True)
        noise = jnp.sum(jnp.where(here, var_ref[batch], 0.0), axis=1, keepdims=True)
        widening = (at + 2).astype(F32)
        inno[i * OBS : (i + 1) * OBS, :] = jnp.broadcast_to(value, (OBS, 128))
        var[i * OBS : (i + 1) * OBS, :] = jnp.broadcast_to(noise * widening, (OBS, 128))


def border(batch, await_rows, y_ref, yh, yl, ah, al, vinv, tref, wref, cross_ref, qref, inno, var):
    corner = lax.broadcasted_iota(jnp.int32, (128, 128), 0) == lax.broadcasted_iota(jnp.int32, (128, 128), 1)
    for s in range(3):
        at = slice(128 * s, 128 * s + 128)
        await_rows(s)

        def centre(i, _):
            rows = pl.ds(pl.multiple_of(s * 128 + i * 32, 32), 32)
            y = y_ref[batch, rows, :]
            mean = jnp.sum(y, axis=1, keepdims=True) * (1.0 / 1024.0)
            yh[rows, :], yl[rows, :] = split(y - mean)
            inno[rows, :] = inno[rows, :] - mean
            return 0

        lax.fori_loop(0, 4, centre, 0)
        high, low = yh[at, :], yl[at, :]
        upto = slice(0, 128 * s + 128)
        total = dot_t(high, yh[upto, :]) + (dot_t(high, yl[upto, :]) + dot_t(low, yh[upto, :]))
        c = [total[:, 128 * i : 128 * i + 128] * (1.0 / 1023.0) for i in range(s + 1)]
        schur = c[s] + jnp.where(corner, var[at, :], 0.0)
        if batch:
            x = cross_of(ah, al, high, low)
        if s == 0:
            if batch:
                cross_ref[:, 0:128] = x
            vinv[0] = inverse128(schur)
        elif s == 1:
            t10 = dot(c[0], vinv[0], HIGHEST)
            tref[...] = t10
            schur = schur - dot_t(t10, c[0], HIGHEST)
            if batch:
                cross_ref[:, 128:256] = x - dot_t(cross_ref[:, 0:128], t10, HIGHEST)
            vinv[1] = inverse128(schur)
            if batch:
                p1 = dot(cross_ref[:, 128:256], vinv[1], HIGHEST)
                qref[:, 128:256] = p1
                qref[:, 0:128] = dot(cross_ref[:, 0:128], vinv[0], HIGHEST) - dot(p1, t10, HIGHEST)
        else:
            t10 = tref[...]
            t20 = dot(c[0], vinv[0], HIGHEST)
            e21 = c[1] - dot_t(c[0], t10, HIGHEST)
            t21 = dot(e21, vinv[1], HIGHEST)
            schur = schur - (dot_t(t20, c[0], HIGHEST) + dot_t(t21, e21, HIGHEST))
            wref[:, 0:128] = t20 - dot(t21, t10, HIGHEST)
            wref[:, 128:256] = t21
            if batch:
                past = dot_t(cross_ref[:, 0:128], t20, HIGHEST) + dot_t(cross_ref[:, 128:256], t21, HIGHEST)
                cross_ref[:, 256:384] = x - past
            vinv[2] = inverse128(schur)


def cross_of(ah, al, high, low):
    a, b = ah[...], al[...]
    return (dot_t(a, high) + (dot_t(a, low) + dot_t(b, high))) * (1.0 / 1023.0)


def anomalies(x_ref, ah, al):
    def anomaly(i, _):
        at = pl.ds(pl.multiple_of(i * 32, 32), 32)
        x = x_ref[at, :]
        ah[at, :], al[at, :] = split(x - jnp.sum(x, axis=1, keepdims=True) * (1.0 / 1024.0))
        return 0

    lax.fori_loop(0, 8, anomaly, 0)


def whole_gain(cross, vinv, tref, wref, gain_ref):
    x0, x1, x2 = (cross[:, 128 * i : 128 * i + 128] for i in range(3))
    t10, w0, w1 = tref[...], wref[:, 0:128], wref[:, 128:256]
    x1 = x1 - dot_t(x0, t10, HIGHEST)
    x2 = x2 - (dot_t(x0, w0, HIGHEST) + dot_t(cross[:, 128:256], w1, HIGHEST))
    p0, p1 = dot(x0, vinv[0], HIGHEST), dot(x1, vinv[1], HIGHEST)
    last = dot(x2, vinv[2], HIGHEST)
    gain_ref[:, 256:384] = last
    gain_ref[:, 128:256] = p1 - dot(last, w1, HIGHEST)
    gain_ref[:, 0:128] = (p0 - dot(p1, t10, HIGHEST)) - dot(last, w0, HIGHEST)


def last_gain(vinv, wref, cross_ref, qref, gain_ref):
    last = dot(cross_ref[:, 256:384], vinv[2], HIGHEST)
    gain_ref[:, 256:384] = last
    gain_ref[:, 0:256] = qref[...] - dot(last, wref[...], HIGHEST)


def whole_kernel(
    state_hbm, cell_hbm, val_hbm, var_hbm, nbr_ref, o_ref,
    state_ref, cell_ref, val_ref, var_ref,
    rows, sbuf, y_ref, xbuf, x_ref, x2_ref, rbuf, tbuf,
    yh, yl, ah, al, vinv, tref, wref, cross_ref, qref, gain_ref, inno, var,
    load_sem, send_sem, recv_sem, xsend_sem, xrecv_sem, asend_sem, arecv_sem, osend_sem, orecv_sem,
):
    region, member, sides = place()
    patch = region * 8 + member
    lane = lax.broadcasted_iota(jnp.int32, (OBS, 256), 1)
    loads = [
        pltpu.make_async_copy(src, dst, load_sem.at[i])
        for i, (src, dst) in enumerate(
            ((state_hbm, state_ref), (cell_hbm, cell_ref), (val_hbm, val_ref), (var_hbm, var_ref))
        )
    ]
    for load in loads:
        load.start()
    peers = all_peers(member, sides)
    barrier = pltpu.get_barrier_semaphore()
    for peer in peers:
        pl.semaphore_signal(barrier, inc=1, device_id=peer, device_id_type=MESH)
    loads[0].wait()
    loads[1].wait()
    for q in range(8):
        cell = jnp.sum(jnp.where(lane == region * 8 + q, cell_ref[0], 0), axis=1, keepdims=True)
        picked = jnp.where(lane == cell, 1.0, 0.0)
        rows[0, q] = dot_t(picked, state_ref[:, q, :], HIGHEST)
    pl.semaphore_wait(barrier, len(peers))

    sent = exchange(0, region, member, sides, nbr_ref, rows, sbuf, y_ref, send_sem, recv_sem)
    for q in range(8):
        xbuf[q] = state_ref[:, q, :].T
    for d in range(1, 8):
        other = lax.rem(member + d, 8)
        copy = remote(xbuf.at[other], x_ref.at[:, columns(member)], xsend_sem.at[d], xrecv_sem.at[member], region, other)
        copy.start()
        sent.append(copy)
    x_ref[:, columns(member)] = xbuf[member]
    loads[2].wait()
    loads[3].wait()
    observed(0, patch, region, sides, nbr_ref, val_ref, var_ref, inno, var)

    def first_rows(s):
        await_side(0, s, member, sides, sbuf, y_ref, send_sem, recv_sem)

    border(0, first_rows, y_ref, yh, yl, ah, al, vinv, tref, wref, cross_ref, qref, inno, var)
    for d in range(1, 8):
        other = lax.rem(member + d, 8)
        remote(xbuf.at[other], x_ref.at[:, columns(other)], xsend_sem.at[d], xrecv_sem.at[other], region, other).wait_recv()

    anomalies(x_ref, ah, al)
    whole_gain(cross_of(ah, al, yh[...], yl[...]), vinv, tref, wref, gain_ref)
    gain = gain_ref[...]
    shift = dot(gain, inno[...], HIGHEST)
    cell = jnp.sum(jnp.where(lane == patch, cell_ref[1], 0), axis=1, keepdims=True)
    picked = jnp.where(lane == cell, 1.0, 0.0)
    pshift = dot(picked, shift, HIGHEST)
    ph, pl_ = split(dot(picked, -0.5 * gain, HIGHEST))
    for d in range(8):
        other = lax.rem(member + d, 8)
        at = columns(other)
        h, l = yh[:, at], yl[:, at]
        r = dot(picked, x_ref[:, at], HIGHEST) + (pshift + (dot(ph, h) + (dot(ph, l) + dot(pl_, h))))
        rbuf[d] = r
        y_ref[1, 0:OBS, at] = r
        if d == 0:
            rows[1, member] = r
            continue
        copy = remote(rbuf.at[d], rows.at[1, member], asend_sem.at[d], arecv_sem.at[member], region, other)
        copy.start()
        sent.append(copy)
    gh, gl = split(-0.5 * gain)
    for i in range(8):
        at = slice(i * 128, i * 128 + 128)
        h, l = yh[:, at], yl[:, at]
        x2_ref[:, at] = x_ref[:, at] + (shift + (dot(gh, h) + (dot(gh, l) + dot(gl, h))))
    observed(1, patch, region, sides, nbr_ref, val_ref, var_ref, inno, var)
    for d in range(1, 8):
        other = lax.rem(member + d, 8)
        remote(rbuf.at[d], rows.at[1, other], asend_sem.at[d], arecv_sem.at[other], region, other).wait_recv()

    sent += exchange(1, region, member, sides, nbr_ref, rows, sbuf, y_ref, send_sem, recv_sem)
    anomalies(x2_ref, ah, al)

    def later_rows(s):
        await_side(1, s, member, sides, sbuf, y_ref, send_sem, recv_sem)

    border(1, later_rows, y_ref, yh, yl, ah, al, vinv, tref, wref, cross_ref, qref, inno, var)
    last_gain(vinv, wref, cross_ref, qref, gain_ref)
    gain = gain_ref[...]
    shift = dot(gain, inno[...], HIGHEST)
    gh, gl = split(-0.5 * gain)
    for d in (1, 2, 3, 4, 5, 6, 7, 0):
        other = lax.rem(member + d, 8)
        at = columns(other)
        h, l = yh[:, at], yl[:, at]
        x = x2_ref[:, at] + (shift + (dot(gh, h) + (dot(gh, l) + dot(gl, h))))
        if d == 0:
            o_ref[member] = x.T
            continue
        tbuf[d] = x.T
        copy = remote(tbuf.at[d], o_ref.at[member], osend_sem.at[d], orecv_sem.at[member], region, other)
        copy.start()
        sent.append(copy)
    for d in range(1, 8):
        other = lax.rem(member + d, 8)
        remote(tbuf.at[d], o_ref.at[other], osend_sem.at[d], orecv_sem.at[other], region, other).wait_recv()
    for copy in sent:
        copy.wait_send()


def on_device(state, neighbours, obs_cell, obs_values, obs_var):
    small = pltpu.VMEM((2, OBS, 256), F32)
    out = pl.pallas_call(
        whole_kernel,
        out_shape=jax.ShapeDtypeStruct((8, 128, 256), F32),
        in_specs=[ANY] * 4 + [SMEM],
        out_specs=VMEM,
        scratch_shapes=[
            pltpu.VMEM((128, 8, 256), F32),
            pltpu.VMEM((2, OBS, 256), jnp.int32),
            small,
            small,
            pltpu.VMEM((2, 8, OBS, 128), F32),
            pltpu.VMEM((2, 3, 8, 128, 128), F32),
            pltpu.VMEM((2, 384, 1024), F32),
            pltpu.VMEM((8, 256, 128), F32),
            pltpu.VMEM((256, 1024), F32),
            pltpu.VMEM((256, 1024), F32),
            pltpu.VMEM((8, OBS, 128), F32),
            pltpu.VMEM((8, 128, 256), F32),
            pltpu.VMEM((384, 1024), BF16),
            pltpu.VMEM((384, 1024), BF16),
            pltpu.VMEM((256, 1024), BF16),
            pltpu.VMEM((256, 1024), BF16),
            pltpu.VMEM((3, 128, 128), F32),
            pltpu.VMEM((128, 128), F32),
            pltpu.VMEM((128, 256), F32),
            pltpu.VMEM((256, 384), F32),
            pltpu.VMEM((256, 256), F32),
            pltpu.VMEM((256, 384), F32),
            pltpu.VMEM((384, 128), F32),
            pltpu.VMEM((384, 128), F32),
            DMA((4,)),
            DMA((2, 3, 8)),
            DMA((2, 3, 8)),
            DMA((8,)),
            DMA((8,)),
            DMA((8,)),
            DMA((8,)),
            DMA((8,)),
            DMA((8,)),
        ],
        compiler_params=pltpu.CompilerParams(
            collective_id=0, has_side_effects=True, vmem_limit_bytes=60 * 1024 * 1024
        ),
        name="whole",
    )(
        state,
        jnp.transpose(obs_cell, (1, 2, 0)),
        jnp.transpose(obs_values, (1, 2, 0)),
        jnp.transpose(obs_var, (1, 2, 0)),
        jnp.transpose(neighbours, (1, 0)),
    )
    return jnp.transpose(out, (1, 0, 2))


def solution(mesh):
    in_specs = (P("member", "region", None), P(), P(), P(), P())
    out_specs = P("member", "region", None)
    return jax.shard_map(on_device, mesh=mesh, in_specs=in_specs, out_specs=out_specs, check_vma=False)
```

```python
import jax
import jax.numpy as jnp
from jax import lax
from jax.experimental import pallas as pl
from jax.experimental.pallas import tpu as pltpu
from jax.sharding import PartitionSpec as P

F32 = jnp.float32
BF16 = jnp.bfloat16
HIGHEST = lax.Precision.HIGHEST
MESH = pl.DeviceIdType.MESH
TILE = (8, 128)
OBS = 64
VMEM = pl.BlockSpec(memory_space=pltpu.VMEM)
SMEM = pl.BlockSpec(memory_space=pltpu.SMEM)
ANY = pl.BlockSpec(memory_space=pl.ANY)
DMA = pltpu.SemaphoreType.DMA


def dot(a, b, precision=None):
    return lax.dot_general(a, b, (((1,), (0,)), ((), ())), precision=precision, preferred_element_type=F32)


def dot_t(a, b, precision=None):
    return lax.dot_general(a, b, (((1,), (1,)), ((), ())), precision=precision, preferred_element_type=F32)


def split(x):
    high = x.astype(BF16)
    return high, (x - high.astype(F32)).astype(BF16)


def spread_tile(x):
    return jnp.broadcast_to(x, TILE)


def solve8(e, r):
    m = {}
    q = [None] * 8
    for i in range(0, 8, 2):
        a, b, d = e[i][i], e[i + 1][i], e[i + 1][i + 1]
        inv = 1.0 / (a * d - b * b)
        ai, bi, di = d * inv, b * inv, a * inv
        for k in range(i + 2, 8):
            m[k, i] = e[k][i] * ai - e[k][i + 1] * bi
            m[k, i + 1] = e[k][i + 1] * di - e[k][i] * bi
        for k in range(i + 2, 8):
            for j in range(i + 2, k + 1):
                e[k][j] = e[k][j] - (m[k, i] * e[j][i] + m[k, i + 1] * e[j][i + 1])
        for k in range(i + 2, 8):
            r[k] = r[k] - (m[k, i] * r[i] + m[k, i + 1] * r[i + 1])
        q[i], q[i + 1] = ai * r[i] - bi * r[i + 1], di * r[i + 1] - bi * r[i]
    for i in range(6, 0, -2):
        for k in range(i):
            q[k] = q[k] - (m[i, k] * q[i] + m[i + 1, k] * q[i + 1])
    return q


def inverse128(block):
    lane = lax.broadcasted_iota(jnp.int32, TILE, 1)
    sub = lax.broadcasted_iota(jnp.int32, TILE, 0)
    front = lax.broadcasted_iota(jnp.int32, (96, 128), 1) < 32

    def strip(_, matrix):
        tiles = [matrix[8 * i : 8 * i + 8, :] for i in range(4)]
        old = matrix[32:, :]
        for t in range(4):
            cols = [[spread_tile(tile[:, 8 * t + k : 8 * t + k + 1]) for k in range(8)] for tile in tiles]
            e = [[spread_tile(cols[t][j][k : k + 1, :]) if j <= k else None for j in range(8)] for k in range(8)]
            inside = (lane >= 8 * t) & (lane < 8 * t + 8)
            rows = [
                jnp.where(lane == 8 * t + k, 1.0, jnp.where(inside, 0.0, spread_tile(tiles[t][k : k + 1, :])))
                for k in range(8)
            ]
            new = solve8(e, rows)
            for i in range(4):
                if i == t:
                    u = new[0]
                    for k in range(1, 8):
                        u = jnp.where(sub == k, new[k], u)
                else:
                    p = [cols[i][k] * new[k] for k in range(8)]
                    u = jnp.where(inside, 0.0, tiles[i])
                    u = u - (((p[0] + p[1]) + (p[2] + p[3])) + ((p[4] + p[5]) + (p[6] + p[7])))
                tiles[i] = u
        top = jnp.concatenate(tiles, axis=0)
        padded = jnp.concatenate([top, jnp.zeros((96, 128), F32)], axis=0)
        fresh = jnp.where(front, 0.0, old) - dot(jnp.where(front, old, 0.0), padded, HIGHEST)
        return pltpu.roll(jnp.concatenate([fresh, top], axis=0), 96, 1)

    return lax.fori_loop(0, 4, strip, block)


def inverse128_unrolled(block):
    lane = lax.broadcasted_iota(jnp.int32, TILE, 1)
    sub = lax.broadcasted_iota(jnp.int32, TILE, 0)
    lanes = lax.broadcasted_iota(jnp.int32, (96, 128), 1)
    tiles = [block[8 * i : 8 * i + 8, :] for i in range(16)]
    for s in range(4):
        mine = list(range(4 * s, 4 * s + 4))
        others = [i for i in range(16) if i not in mine]
        old = jnp.concatenate([tiles[i] for i in others], axis=0)
        for t in mine:
            cols = {i: [spread_tile(tiles[i][:, 8 * t + k : 8 * t + k + 1]) for k in range(8)] for i in mine}
            e = [[spread_tile(cols[t][j][k : k + 1, :]) if j <= k else None for j in range(8)] for k in range(8)]
            inside = (lane >= 8 * t) & (lane < 8 * t + 8)
            rows = [
                jnp.where(lane == 8 * t + k, 1.0, jnp.where(inside, 0.0, spread_tile(tiles[t][k : k + 1, :])))
                for k in range(8)
            ]
            new = solve8(e, rows)
            for i in mine:
                if i == t:
                    u = new[0]
                    for k in range(1, 8):
                        u = jnp.where(sub == k, new[k], u)
                else:
                    u = jnp.where(inside, 0.0, tiles[i])
                    p = [cols[i][k] * new[k] for k in range(8)]
                    u = u - (((p[0] + p[1]) + (p[2] + p[3])) + ((p[4] + p[5]) + (p[6] + p[7])))
                tiles[i] = u
        low, high = 32 * s, 32 * s + 32
        parts = [jnp.concatenate([tiles[i] for i in mine], axis=0)]
        if low:
            parts.insert(0, jnp.zeros((low, 128), F32))
        if high < 128:
            parts.append(jnp.zeros((128 - high, 128), F32))
        strip = jnp.concatenate(parts, axis=0)
        inside = (lanes >= low) & (lanes < high)
        fresh = jnp.where(inside, 0.0, old) - dot(jnp.where(inside, old, 0.0), strip, HIGHEST)
        for q, i in enumerate(others):
            tiles[i] = fresh[8 * q : 8 * q + 8]
    return jnp.concatenate(tiles, axis=0)


def linked(nbr_ref, patch, home):
    first = last = first_at = last_at = jnp.int32(0)
    for j in range(5):
        n = nbr_ref[j, patch]
        here = (n >> 3) == home
        last = jnp.where(here, n, last)
        last_at = jnp.where(here, j, last_at)
    for j in reversed(range(5)):
        n = nbr_ref[j, patch]
        here = (n >> 3) == home
        first = jnp.where(here, n, first)
        first_at = jnp.where(here, j, first_at)
    return first, first_at, last, last_at


def place():
    region, member = lax.axis_index("region"), lax.axis_index("member")
    regions = lax.axis_size("region")
    sides = (region, lax.rem(region + 1, regions), lax.rem(region + regions - 1, regions))
    return region, member, sides


def columns(member):
    return pl.ds(pl.multiple_of(member * 128, 128), 128)


def all_peers(member, sides):
    return [
        {"region": sides[s], "member": lax.rem(member + d, 8)}
        for d in range(8)
        for s in range(3)
        if (s, d) != (0, 0)
    ]


def remote(src, dst, send, recv, region, member):
    return pltpu.make_async_remote_copy(
        src_ref=src,
        dst_ref=dst,
        send_sem=send,
        recv_sem=recv,
        device_id={"region": region, "member": member},
        device_id_type=MESH,
    )


def start_of(batch, s):
    return OBS if batch and s == 0 else 0


def exchange(batch, region, member, sides, nbr_ref, rows, sbuf, y_ref, send_sem, recv_sem):
    sent = []
    for s in range(3):
        start = start_of(batch, s)
        for d in range(8):
            other = lax.rem(member + d, 8)
            first, _, last, _ = linked(nbr_ref, sides[s] * 8 + other, region)
            if s == 0:
                if batch == 0:
                    sbuf[batch, s, d, 0:OBS, :] = rows[batch, other]
                sbuf[batch, s, d, OBS : 2 * OBS, :] = rows[batch, first & 7]
            else:
                sbuf[batch, s, d, 0:OBS, :] = rows[batch, first & 7]
                sbuf[batch, s, d, OBS : 2 * OBS, :] = rows[batch, last & 7]
            if s == 0 and d == 0:
                y_ref[batch, start : 2 * OBS, columns(member)] = sbuf[batch, 0, 0, start : 2 * OBS, :]
                continue
            copy = remote(
                sbuf.at[batch, s, d, pl.ds(start, 2 * OBS - start)],
                y_ref.at[batch, pl.ds(s * 128 + start, 2 * OBS - start), columns(member)],
                send_sem.at[batch, s, d],
                recv_sem.at[batch, s, member],
                sides[s],
                other,
            )
            copy.start()
            sent.append(copy)
    return sent


def await_side(batch, s, member, sides, sbuf, y_ref, send_sem, recv_sem):
    start = start_of(batch, s)
    for d in range(8):
        if (s, d) == (0, 0):
            continue
        other = lax.rem(member + d, 8)
        remote(
            sbuf.at[batch, s, d, pl.ds(start, 2 * OBS - start)],
            y_ref.at[batch, pl.ds(s * 128 + start, 2 * OBS - start), columns(other)],
            send_sem.at[batch, s, d],
            recv_sem.at[batch, s, other],
            sides[s],
            other,
        ).wait_recv()


def observed(batch, patch, region, sides, nbr_ref, val_ref, var_ref, inno, var):
    lane = lax.broadcasted_iota(jnp.int32, (OBS, 256), 1)
    same, same_at, _, _ = linked(nbr_ref, patch, region)
    slots = [(patch, jnp.int32(-1)), (same, same_at)]
    for side in (sides[2], sides[1]):
        f, fa, l, la = linked(nbr_ref, patch, side)
        slots += [(f, fa), (l, la)]
    for i, (n, at) in enumerate(slots):
        here = lane == n
        value = jnp.sum(jnp.where(here, val_ref[batch], 0.0), axis=1, keepdims=True)
        noise = jnp.sum(jnp.where(here, var_ref[batch], 0.0), axis=1, keepdims=True)
        widening = (at + 2).astype(F32)
        inno[i * OBS : (i + 1) * OBS, :] = jnp.broadcast_to(value, (OBS, 128))
        var[i * OBS : (i + 1) * OBS, :] = jnp.broadcast_to(noise * widening, (OBS, 128))


def border(batch, await_rows, y_ref, yh, yl, ah, al, vinv, tref, wref, cross_ref, qref, inno, var):
    corner = lax.broadcasted_iota(jnp.int32, (128, 128), 0) == lax.broadcasted_iota(jnp.int32, (128, 128), 1)
    inverse = inverse128_unrolled if batch else inverse128
    for s in range(3):
        at = slice(128 * s, 128 * s + 128)
        await_rows(s)

        def centre(i, _):
            rows = pl.ds(pl.multiple_of(s * 128 + i * 32, 32), 32)
            y = y_ref[batch, rows, :]
            mean = jnp.sum(y, axis=1, keepdims=True) * (1.0 / 1024.0)
            yh[rows, :], yl[rows, :] = split(y - mean)
            inno[rows, :] = inno[rows, :] - mean
            return 0

        lax.fori_loop(0, 4, centre, 0)
        high, low = yh[at, :], yl[at, :]
        upto = slice(0, 128 * s + 128)
        total = dot_t(high, yh[upto, :]) + (dot_t(high, yl[upto, :]) + dot_t(low, yh[upto, :]))
        c = [total[:, 128 * i : 128 * i + 128] * (1.0 / 1023.0) for i in range(s + 1)]
        schur = c[s] + jnp.where(corner, var[at, :], 0.0)
        if batch:
            x = cross_of(ah, al, high, low)
        if s == 0:
            if batch:
                cross_ref[:, 0:128] = x
            vinv[0] = inverse(schur)
        elif s == 1:
            t10 = dot(c[0], vinv[0], HIGHEST)
            tref[...] = t10
            schur = schur - dot_t(t10, c[0], HIGHEST)
            if batch:
                cross_ref[:, 128:256] = x - dot_t(cross_ref[:, 0:128], t10, HIGHEST)
            vinv[1] = inverse(schur)
            if batch:
                p1 = dot(cross_ref[:, 128:256], vinv[1], HIGHEST)
                qref[:, 128:256] = p1
                qref[:, 0:128] = dot(cross_ref[:, 0:128], vinv[0], HIGHEST) - dot(p1, t10, HIGHEST)
        else:
            t10 = tref[...]
            t20 = dot(c[0], vinv[0], HIGHEST)
            e21 = c[1] - dot_t(c[0], t10, HIGHEST)
            t21 = dot(e21, vinv[1], HIGHEST)
            schur = schur - (dot_t(t20, c[0], HIGHEST) + dot_t(t21, e21, HIGHEST))
            wref[:, 0:128] = t20 - dot(t21, t10, HIGHEST)
            wref[:, 128:256] = t21
            if batch:
                past = dot_t(cross_ref[:, 0:128], t20, HIGHEST) + dot_t(cross_ref[:, 128:256], t21, HIGHEST)
                cross_ref[:, 256:384] = x - past
            vinv[2] = inverse(schur)


def cross_of(ah, al, high, low):
    a, b = ah[...], al[...]
    return (dot_t(a, high) + (dot_t(a, low) + dot_t(b, high))) * (1.0 / 1023.0)


def whole_gain(cross, vinv, tref, wref, gain_ref):
    x0, x1, x2 = (cross[:, 128 * i : 128 * i + 128] for i in range(3))
    t10, w0, w1 = tref[...], wref[:, 0:128], wref[:, 128:256]
    x1 = x1 - dot_t(x0, t10, HIGHEST)
    x2 = x2 - (dot_t(x0, w0, HIGHEST) + dot_t(cross[:, 128:256], w1, HIGHEST))
    p0, p1 = dot(x0, vinv[0], HIGHEST), dot(x1, vinv[1], HIGHEST)
    last = dot(x2, vinv[2], HIGHEST)
    gain_ref[:, 256:384] = last
    gain_ref[:, 128:256] = p1 - dot(last, w1, HIGHEST)
    gain_ref[:, 0:128] = (p0 - dot(p1, t10, HIGHEST)) - dot(last, w0, HIGHEST)


def last_gain(vinv, wref, cross_ref, qref, gain_ref):
    last = dot(cross_ref[:, 256:384], vinv[2], HIGHEST)
    gain_ref[:, 256:384] = last
    gain_ref[:, 0:256] = qref[...] - dot(last, wref[...], HIGHEST)


def whole_kernel(
    state_hbm, cell_hbm, val_hbm, var_hbm, nbr_ref, o_ref,
    state_ref, cell_ref, val_ref, var_ref,
    rows, sbuf, y_ref, xbuf, x_ref, x2_ref, rbuf, tbuf,
    yh, yl, ah, al, vinv, tref, wref, cross_ref, qref, gain_ref, inno, var,
    load_sem, send_sem, recv_sem, xsend_sem, xrecv_sem, asend_sem, arecv_sem, osend_sem, orecv_sem,
):
    region, member, sides = place()
    patch = region * 8 + member
    lane = lax.broadcasted_iota(jnp.int32, (OBS, 256), 1)
    loads = [
        pltpu.make_async_copy(src, dst, load_sem.at[i])
        for i, (src, dst) in enumerate(
            ((state_hbm, state_ref), (cell_hbm, cell_ref), (val_hbm, val_ref), (var_hbm, var_ref))
        )
    ]
    for load in loads:
        load.start()
    peers = all_peers(member, sides)
    barrier = pltpu.get_barrier_semaphore()
    for peer in peers:
        pl.semaphore_signal(barrier, inc=1, device_id=peer, device_id_type=MESH)
    loads[0].wait()
    loads[1].wait()
    for q in range(8):
        cell = jnp.sum(jnp.where(lane == region * 8 + q, cell_ref[0], 0), axis=1, keepdims=True)
        picked = jnp.where(lane == cell, 1.0, 0.0)
        rows[0, q] = dot_t(picked, state_ref[:, q, :], HIGHEST)
    pl.semaphore_wait(barrier, len(peers))

    sent = exchange(0, region, member, sides, nbr_ref, rows, sbuf, y_ref, send_sem, recv_sem)
    for q in range(8):
        xbuf[q] = state_ref[:, q, :].T
    for d in range(1, 8):
        other = lax.rem(member + d, 8)
        copy = remote(xbuf.at[other], x_ref.at[:, columns(member)], xsend_sem.at[d], xrecv_sem.at[member], region, other)
        copy.start()
        sent.append(copy)
    x_ref[:, columns(member)] = xbuf[member]
    loads[2].wait()
    loads[3].wait()
    observed(0, patch, region, sides, nbr_ref, val_ref, var_ref, inno, var)

    def first_rows(s):
        await_side(0, s, member, sides, sbuf, y_ref, send_sem, recv_sem)

    border(0, first_rows, y_ref, yh, yl, ah, al, vinv, tref, wref, cross_ref, qref, inno, var)
    for d in range(8):
        other = lax.rem(member + 8 - d, 8)
        at = columns(other)
        if d:
            remote(xbuf.at[other], x_ref.at[:, at], xsend_sem.at[d], xrecv_sem.at[other], region, other).wait_recv()
        high, low = split(x_ref[:, at])
        ah[:, at], al[:, at] = high, low
        part = dot_t(high, yh[:, at]) + (dot_t(high, yl[:, at]) + dot_t(low, yh[:, at]))
        cross_ref[...] = cross_ref[...] + part if d else part

    whole_gain(cross_ref[...] * (1.0 / 1023.0), vinv, tref, wref, gain_ref)
    gain = gain_ref[...]
    shift = dot(gain, inno[...], HIGHEST)
    cell = jnp.sum(jnp.where(lane == patch, cell_ref[1], 0), axis=1, keepdims=True)
    picked = jnp.where(lane == cell, 1.0, 0.0)
    chosen = picked.astype(BF16)
    pshift = dot(picked, shift, HIGHEST)
    ph, pl_ = split(dot(picked, -0.5 * gain, HIGHEST))
    for d in (1, 2, 3, 4, 5, 6, 7, 0):
        other = lax.rem(member + d, 8)
        at = columns(other)
        h, l = yh[:, at], yl[:, at]
        r = (dot(chosen, ah[:, at]) + dot(chosen, al[:, at])) + (pshift + (dot(ph, h) + (dot(ph, l) + dot(pl_, h))))
        rbuf[d] = r
        y_ref[1, 0:OBS, at] = r
        if d == 0:
            rows[1, member] = r
            continue
        copy = remote(rbuf.at[d], rows.at[1, member], asend_sem.at[d], arecv_sem.at[member], region, other)
        copy.start()
        sent.append(copy)
    gh, gl = split(-0.5 * gain)
    for i in range(8):
        at = slice(i * 128, i * 128 + 128)
        h, l = yh[:, at], yl[:, at]
        x = x_ref[:, at] + (shift + (dot(gh, h) + (dot(gh, l) + dot(gl, h))))
        x2_ref[:, at] = x
        ah[:, at], al[:, at] = split(x)
    observed(1, patch, region, sides, nbr_ref, val_ref, var_ref, inno, var)
    for d in range(1, 8):
        other = lax.rem(member + d, 8)
        remote(rbuf.at[d], rows.at[1, other], asend_sem.at[d], arecv_sem.at[other], region, other).wait_recv()

    sent += exchange(1, region, member, sides, nbr_ref, rows, sbuf, y_ref, send_sem, recv_sem)

    def later_rows(s):
        await_side(1, s, member, sides, sbuf, y_ref, send_sem, recv_sem)

    border(1, later_rows, y_ref, yh, yl, ah, al, vinv, tref, wref, cross_ref, qref, inno, var)
    last_gain(vinv, wref, cross_ref, qref, gain_ref)
    gain = gain_ref[...]
    shift = dot(gain, inno[...], HIGHEST)
    gh, gl = split(-0.5 * gain)
    for d in (1, 2, 3, 4, 5, 6, 7, 0):
        other = lax.rem(member + d, 8)
        at = columns(other)
        h, l = yh[:, at], yl[:, at]
        x = x2_ref[:, at] + (shift + (dot(gh, h) + (dot(gh, l) + dot(gl, h))))
        if d == 0:
            o_ref[member] = x.T
            continue
        tbuf[d] = x.T
        copy = remote(tbuf.at[d], o_ref.at[member], osend_sem.at[d], orecv_sem.at[member], region, other)
        copy.start()
        sent.append(copy)
    for d in range(1, 8):
        other = lax.rem(member + d, 8)
        remote(tbuf.at[d], o_ref.at[other], osend_sem.at[d], orecv_sem.at[other], region, other).wait_recv()
    for copy in sent:
        copy.wait_send()


def on_device(state, neighbours, obs_cell, obs_values, obs_var):
    small = pltpu.VMEM((2, OBS, 256), F32)
    out = pl.pallas_call(
        whole_kernel,
        out_shape=jax.ShapeDtypeStruct((8, 128, 256), F32),
        in_specs=[ANY] * 4 + [SMEM],
        out_specs=VMEM,
        scratch_shapes=[
            pltpu.VMEM((128, 8, 256), F32),
            pltpu.VMEM((2, OBS, 256), jnp.int32),
            small,
            small,
            pltpu.VMEM((2, 8, OBS, 128), F32),
            pltpu.VMEM((2, 3, 8, 128, 128), F32),
            pltpu.VMEM((2, 384, 1024), F32),
            pltpu.VMEM((8, 256, 128), F32),
            pltpu.VMEM((256, 1024), F32),
            pltpu.VMEM((256, 1024), F32),
            pltpu.VMEM((8, OBS, 128), F32),
            pltpu.VMEM((8, 128, 256), F32),
            pltpu.VMEM((384, 1024), BF16),
            pltpu.VMEM((384, 1024), BF16),
            pltpu.VMEM((256, 1024), BF16),
            pltpu.VMEM((256, 1024), BF16),
            pltpu.VMEM((3, 128, 128), F32),
            pltpu.VMEM((128, 128), F32),
            pltpu.VMEM((128, 256), F32),
            pltpu.VMEM((256, 384), F32),
            pltpu.VMEM((256, 256), F32),
            pltpu.VMEM((256, 384), F32),
            pltpu.VMEM((384, 128), F32),
            pltpu.VMEM((384, 128), F32),
            DMA((4,)),
            DMA((2, 3, 8)),
            DMA((2, 3, 8)),
            DMA((8,)),
            DMA((8,)),
            DMA((8,)),
            DMA((8,)),
            DMA((8,)),
            DMA((8,)),
        ],
        compiler_params=pltpu.CompilerParams(
            collective_id=0, has_side_effects=True, vmem_limit_bytes=60 * 1024 * 1024
        ),
        name="whole",
    )(
        state,
        jnp.transpose(obs_cell, (1, 2, 0)),
        jnp.transpose(obs_values, (1, 2, 0)),
        jnp.transpose(obs_var, (1, 2, 0)),
        jnp.transpose(neighbours, (1, 0)),
    )
    return jnp.transpose(out, (1, 0, 2))


def solution(mesh):
    in_specs = (P("member", "region", None), P(), P(), P(), P())
    out_specs = P("member", "region", None)
    return jax.shard_map(on_device, mesh=mesh, in_specs=in_specs, out_specs=out_specs, check_vma=False)
```

```python
import jax
import jax.numpy as jnp
from jax import lax
from jax.experimental import pallas as pl
from jax.experimental.pallas import tpu as pltpu
from jax.sharding import PartitionSpec as P

F32 = jnp.float32
BF16 = jnp.bfloat16
HIGHEST = lax.Precision.HIGHEST
MESH = pl.DeviceIdType.MESH
TILE = (8, 128)
OBS = 64
VMEM = pl.BlockSpec(memory_space=pltpu.VMEM)
SMEM = pl.BlockSpec(memory_space=pltpu.SMEM)
ANY = pl.BlockSpec(memory_space=pl.ANY)
DMA = pltpu.SemaphoreType.DMA


def dot(a, b, precision=None):
    return lax.dot_general(a, b, (((1,), (0,)), ((), ())), precision=precision, preferred_element_type=F32)


def dot_t(a, b, precision=None):
    return lax.dot_general(a, b, (((1,), (1,)), ((), ())), precision=precision, preferred_element_type=F32)


def split(x):
    high = x.astype(BF16)
    return high, (x - high.astype(F32)).astype(BF16)


def spread_tile(x):
    return jnp.broadcast_to(x, TILE)


def solve8(e, r):
    m = {}
    q = [None] * 8
    for i in range(0, 8, 2):
        a, b, d = e[i][i], e[i + 1][i], e[i + 1][i + 1]
        inv = 1.0 / (a * d - b * b)
        ai, bi, di = d * inv, b * inv, a * inv
        for k in range(i + 2, 8):
            m[k, i] = e[k][i] * ai - e[k][i + 1] * bi
            m[k, i + 1] = e[k][i + 1] * di - e[k][i] * bi
        for k in range(i + 2, 8):
            for j in range(i + 2, k + 1):
                e[k][j] = e[k][j] - (m[k, i] * e[j][i] + m[k, i + 1] * e[j][i + 1])
        for k in range(i + 2, 8):
            r[k] = r[k] - (m[k, i] * r[i] + m[k, i + 1] * r[i + 1])
        q[i], q[i + 1] = ai * r[i] - bi * r[i + 1], di * r[i + 1] - bi * r[i]
    for i in range(6, 0, -2):
        for k in range(i):
            q[k] = q[k] - (m[i, k] * q[i] + m[i + 1, k] * q[i + 1])
    return q


def inverse128(block):
    lane = lax.broadcasted_iota(jnp.int32, TILE, 1)
    sub = lax.broadcasted_iota(jnp.int32, TILE, 0)
    front = lax.broadcasted_iota(jnp.int32, (96, 128), 1) < 32

    def strip(_, matrix):
        tiles = [matrix[8 * i : 8 * i + 8, :] for i in range(4)]
        old = matrix[32:, :]
        for t in range(4):
            cols = [[spread_tile(tile[:, 8 * t + k : 8 * t + k + 1]) for k in range(8)] for tile in tiles]
            e = [[spread_tile(cols[t][j][k : k + 1, :]) if j <= k else None for j in range(8)] for k in range(8)]
            inside = (lane >= 8 * t) & (lane < 8 * t + 8)
            rows = [
                jnp.where(lane == 8 * t + k, 1.0, jnp.where(inside, 0.0, spread_tile(tiles[t][k : k + 1, :])))
                for k in range(8)
            ]
            new = solve8(e, rows)
            for i in range(4):
                if i == t:
                    u = new[0]
                    for k in range(1, 8):
                        u = jnp.where(sub == k, new[k], u)
                else:
                    p = [cols[i][k] * new[k] for k in range(8)]
                    u = jnp.where(inside, 0.0, tiles[i])
                    u = u - (((p[0] + p[1]) + (p[2] + p[3])) + ((p[4] + p[5]) + (p[6] + p[7])))
                tiles[i] = u
        top = jnp.concatenate(tiles, axis=0)
        padded = jnp.concatenate([top, jnp.zeros((96, 128), F32)], axis=0)
        fresh = jnp.where(front, 0.0, old) - dot(jnp.where(front, old, 0.0), padded, HIGHEST)
        return pltpu.roll(jnp.concatenate([fresh, top], axis=0), 96, 1)

    return lax.fori_loop(0, 4, strip, block)


def inverse128_unrolled(block):
    lane = lax.broadcasted_iota(jnp.int32, TILE, 1)
    sub = lax.broadcasted_iota(jnp.int32, TILE, 0)
    lanes = lax.broadcasted_iota(jnp.int32, (96, 128), 1)
    tiles = [block[8 * i : 8 * i + 8, :] for i in range(16)]
    for s in range(4):
        mine = list(range(4 * s, 4 * s + 4))
        others = [i for i in range(16) if i not in mine]
        old = jnp.concatenate([tiles[i] for i in others], axis=0)
        for t in mine:
            cols = {i: [spread_tile(tiles[i][:, 8 * t + k : 8 * t + k + 1]) for k in range(8)] for i in mine}
            e = [[spread_tile(cols[t][j][k : k + 1, :]) if j <= k else None for j in range(8)] for k in range(8)]
            inside = (lane >= 8 * t) & (lane < 8 * t + 8)
            rows = [
                jnp.where(lane == 8 * t + k, 1.0, jnp.where(inside, 0.0, spread_tile(tiles[t][k : k + 1, :])))
                for k in range(8)
            ]
            new = solve8(e, rows)
            for i in mine:
                if i == t:
                    u = new[0]
                    for k in range(1, 8):
                        u = jnp.where(sub == k, new[k], u)
                else:
                    u = jnp.where(inside, 0.0, tiles[i])
                    p = [cols[i][k] * new[k] for k in range(8)]
                    u = u - (((p[0] + p[1]) + (p[2] + p[3])) + ((p[4] + p[5]) + (p[6] + p[7])))
                tiles[i] = u
        low, high = 32 * s, 32 * s + 32
        parts = [jnp.concatenate([tiles[i] for i in mine], axis=0)]
        if low:
            parts.insert(0, jnp.zeros((low, 128), F32))
        if high < 128:
            parts.append(jnp.zeros((128 - high, 128), F32))
        strip = jnp.concatenate(parts, axis=0)
        inside = (lanes >= low) & (lanes < high)
        fresh = jnp.where(inside, 0.0, old) - dot(jnp.where(inside, old, 0.0), strip, HIGHEST)
        for q, i in enumerate(others):
            tiles[i] = fresh[8 * q : 8 * q + 8]
    return jnp.concatenate(tiles, axis=0)


def linked(nbr_ref, patch, home):
    first = last = first_at = last_at = jnp.int32(0)
    for j in range(5):
        n = nbr_ref[j, patch]
        here = (n >> 3) == home
        last = jnp.where(here, n, last)
        last_at = jnp.where(here, j, last_at)
    for j in reversed(range(5)):
        n = nbr_ref[j, patch]
        here = (n >> 3) == home
        first = jnp.where(here, n, first)
        first_at = jnp.where(here, j, first_at)
    return first, first_at, last, last_at


def place():
    region, member = lax.axis_index("region"), lax.axis_index("member")
    regions = lax.axis_size("region")
    sides = (region, lax.rem(region + 1, regions), lax.rem(region + regions - 1, regions))
    return region, member, sides


def columns(member):
    return pl.ds(pl.multiple_of(member * 128, 128), 128)


def all_peers(member, sides):
    return [
        {"region": sides[s], "member": lax.rem(member + d, 8)}
        for d in range(8)
        for s in range(3)
        if (s, d) != (0, 0)
    ]


def remote(src, dst, send, recv, region, member):
    return pltpu.make_async_remote_copy(
        src_ref=src,
        dst_ref=dst,
        send_sem=send,
        recv_sem=recv,
        device_id={"region": region, "member": member},
        device_id_type=MESH,
    )


def start_of(batch, s):
    return OBS if batch and s == 0 else 0


def exchange(batch, picks, member, sides, rows, sbuf, y_ref, send_sem, recv_sem):
    sent = []
    for s in range(3):
        start = start_of(batch, s)
        for d in range(8):
            other = lax.rem(member + d, 8)
            first, last = picks[s][d]
            if s == 0:
                if batch == 0:
                    sbuf[batch, s, d, 0:OBS, :] = rows[batch, other]
                sbuf[batch, s, d, OBS : 2 * OBS, :] = rows[batch, first]
            else:
                sbuf[batch, s, d, 0:OBS, :] = rows[batch, first]
                sbuf[batch, s, d, OBS : 2 * OBS, :] = rows[batch, last]
            if s == 0 and d == 0:
                y_ref[batch, start : 2 * OBS, columns(member)] = sbuf[batch, 0, 0, start : 2 * OBS, :]
                continue
            copy = remote(
                sbuf.at[batch, s, d, pl.ds(start, 2 * OBS - start)],
                y_ref.at[batch, pl.ds(s * 128 + start, 2 * OBS - start), columns(member)],
                send_sem.at[batch, s, d],
                recv_sem.at[batch, s, member],
                sides[s],
                other,
            )
            copy.start()
            sent.append(copy)
    return sent


def await_side(batch, s, member, sides, sbuf, y_ref, send_sem, recv_sem):
    start = start_of(batch, s)
    for d in range(8):
        if (s, d) == (0, 0):
            continue
        other = lax.rem(member + d, 8)
        remote(
            sbuf.at[batch, s, d, pl.ds(start, 2 * OBS - start)],
            y_ref.at[batch, pl.ds(s * 128 + start, 2 * OBS - start), columns(other)],
            send_sem.at[batch, s, d],
            recv_sem.at[batch, s, other],
            sides[s],
            other,
        ).wait_recv()


def observed(batch, patch, region, sides, nbr_ref, val_ref, var_ref, inno, var):
    lane = lax.broadcasted_iota(jnp.int32, (OBS, 256), 1)
    same, same_at, _, _ = linked(nbr_ref, patch, region)
    slots = [(patch, jnp.int32(-1)), (same, same_at)]
    for side in (sides[2], sides[1]):
        f, fa, l, la = linked(nbr_ref, patch, side)
        slots += [(f, fa), (l, la)]
    for i, (n, at) in enumerate(slots):
        here = lane == n
        value = jnp.sum(jnp.where(here, val_ref[batch], 0.0), axis=1, keepdims=True)
        noise = jnp.sum(jnp.where(here, var_ref[batch], 0.0), axis=1, keepdims=True)
        widening = (at + 2).astype(F32)
        inno[i * OBS : (i + 1) * OBS, :] = jnp.broadcast_to(value, (OBS, 128))
        var[i * OBS : (i + 1) * OBS, :] = jnp.broadcast_to(noise * widening, (OBS, 128))


def border(batch, await_rows, y_ref, yh, yl, ah, al, vinv, tref, wref, cross_ref, qref, inno, var):
    corner = lax.broadcasted_iota(jnp.int32, (128, 128), 0) == lax.broadcasted_iota(jnp.int32, (128, 128), 1)
    inverse = inverse128_unrolled if batch else inverse128
    for s in range(3):
        at = slice(128 * s, 128 * s + 128)
        await_rows(s)

        def centre(i, _):
            rows = pl.ds(pl.multiple_of(s * 128 + i * 32, 32), 32)
            y = y_ref[batch, rows, :]
            mean = jnp.sum(y, axis=1, keepdims=True) * (1.0 / 1024.0)
            yh[rows, :], yl[rows, :] = split(y - mean)
            inno[rows, :] = inno[rows, :] - mean
            return 0

        lax.fori_loop(0, 4, centre, 0)
        high, low = yh[at, :], yl[at, :]
        upto = slice(0, 128 * s + 128)
        total = dot_t(high, yh[upto, :]) + (dot_t(high, yl[upto, :]) + dot_t(low, yh[upto, :]))
        c = [total[:, 128 * i : 128 * i + 128] * (1.0 / 1023.0) for i in range(s + 1)]
        schur = c[s] + jnp.where(corner, var[at, :], 0.0)
        if batch:
            x = cross_of(ah, al, high, low)
        if s == 0:
            if batch:
                cross_ref[:, 0:128] = x
            vinv[0] = inverse(schur)
        elif s == 1:
            t10 = dot(c[0], vinv[0], HIGHEST)
            tref[...] = t10
            schur = schur - dot_t(t10, c[0], HIGHEST)
            if batch:
                cross_ref[:, 128:256] = x - dot_t(cross_ref[:, 0:128], t10, HIGHEST)
            vinv[1] = inverse(schur)
            if batch:
                p1 = dot(cross_ref[:, 128:256], vinv[1], HIGHEST)
                qref[:, 128:256] = p1
                qref[:, 0:128] = dot(cross_ref[:, 0:128], vinv[0], HIGHEST) - dot(p1, t10, HIGHEST)
        else:
            t10 = tref[...]
            t20 = dot(c[0], vinv[0], HIGHEST)
            e21 = c[1] - dot_t(c[0], t10, HIGHEST)
            t21 = dot(e21, vinv[1], HIGHEST)
            schur = schur - (dot_t(t20, c[0], HIGHEST) + dot_t(t21, e21, HIGHEST))
            wref[:, 0:128] = t20 - dot(t21, t10, HIGHEST)
            wref[:, 128:256] = t21
            if batch:
                past = dot_t(cross_ref[:, 0:128], t20, HIGHEST) + dot_t(cross_ref[:, 128:256], t21, HIGHEST)
                cross_ref[:, 256:384] = x - past
            vinv[2] = inverse(schur)


def cross_of(ah, al, high, low):
    a, b = ah[...], al[...]
    return (dot_t(a, high) + (dot_t(a, low) + dot_t(b, high))) * (1.0 / 1023.0)


def whole_gain(cross, vinv, tref, wref, gain_ref):
    x0, x1, x2 = (cross[:, 128 * i : 128 * i + 128] for i in range(3))
    t10, w0, w1 = tref[...], wref[:, 0:128], wref[:, 128:256]
    x1 = x1 - dot_t(x0, t10, HIGHEST)
    x2 = x2 - (dot_t(x0, w0, HIGHEST) + dot_t(cross[:, 128:256], w1, HIGHEST))
    p0, p1 = dot(x0, vinv[0], HIGHEST), dot(x1, vinv[1], HIGHEST)
    last = dot(x2, vinv[2], HIGHEST)
    gain_ref[:, 256:384] = last
    gain_ref[:, 128:256] = p1 - dot(last, w1, HIGHEST)
    gain_ref[:, 0:128] = (p0 - dot(p1, t10, HIGHEST)) - dot(last, w0, HIGHEST)


def last_gain(vinv, wref, cross_ref, qref, gain_ref):
    last = dot(cross_ref[:, 256:384], vinv[2], HIGHEST)
    gain_ref[:, 256:384] = last
    gain_ref[:, 0:256] = qref[...] - dot(last, wref[...], HIGHEST)


def whole_kernel(
    state_hbm, cell_hbm, val_hbm, var_hbm, nbr_ref, out_ref,
    state_ref, cell_ref, val_ref, var_ref,
    rows, sbuf, y_ref, xbuf, x_ref, x2_ref, rbuf, tbuf, o_ref,
    yh, yl, ah, al, vinv, tref, wref, cross_ref, qref, gain_ref, inno, var,
    load_sem, send_sem, recv_sem, xsend_sem, xrecv_sem, asend_sem, arecv_sem, osend_sem, orecv_sem,
):
    region, member, sides = place()
    patch = region * 8 + member
    lane = lax.broadcasted_iota(jnp.int32, (OBS, 256), 1)
    loads = [
        pltpu.make_async_copy(src, dst, load_sem.at[i])
        for i, (src, dst) in enumerate(
            ((state_hbm, state_ref), (cell_hbm, cell_ref), (val_hbm, val_ref), (var_hbm, var_ref))
        )
    ]
    for load in loads:
        load.start()
    peers = all_peers(member, sides)
    barrier = pltpu.get_barrier_semaphore()
    for peer in peers:
        pl.semaphore_signal(barrier, inc=1, device_id=peer, device_id_type=MESH)
    picks = [[], [], []]
    for s in range(3):
        for d in range(8):
            first, _, last, _ = linked(nbr_ref, sides[s] * 8 + lax.rem(member + d, 8), region)
            picks[s].append((first & 7, last & 7))
    loads[0].wait()
    loads[1].wait()
    for q in range(8):
        cell = jnp.sum(jnp.where(lane == region * 8 + q, cell_ref[0], 0), axis=1, keepdims=True)
        picked = jnp.where(lane == cell, 1.0, 0.0)
        rows[0, q] = dot_t(picked, state_ref[:, q, :], HIGHEST)
    pl.semaphore_wait(barrier, len(peers))

    sent = exchange(0, picks, member, sides, rows, sbuf, y_ref, send_sem, recv_sem)
    for q in range(8):
        xbuf[q] = state_ref[:, q, :].T
    for d in range(1, 8):
        other = lax.rem(member + d, 8)
        copy = remote(xbuf.at[other], x_ref.at[:, columns(member)], xsend_sem.at[d], xrecv_sem.at[member], region, other)
        copy.start()
        sent.append(copy)
    x_ref[:, columns(member)] = xbuf[member]
    loads[2].wait()
    loads[3].wait()
    observed(0, patch, region, sides, nbr_ref, val_ref, var_ref, inno, var)

    def first_rows(s):
        await_side(0, s, member, sides, sbuf, y_ref, send_sem, recv_sem)

    border(0, first_rows, y_ref, yh, yl, ah, al, vinv, tref, wref, cross_ref, qref, inno, var)
    for d in range(8):
        other = lax.rem(member + 8 - d, 8)
        at = columns(other)
        if d:
            remote(xbuf.at[other], x_ref.at[:, at], xsend_sem.at[d], xrecv_sem.at[other], region, other).wait_recv()
        high, low = split(x_ref[:, at])
        ah[:, at], al[:, at] = high, low
        part = dot_t(high, yh[:, at]) + (dot_t(high, yl[:, at]) + dot_t(low, yh[:, at]))
        cross_ref[...] = cross_ref[...] + part if d else part

    whole_gain(cross_ref[...] * (1.0 / 1023.0), vinv, tref, wref, gain_ref)
    gain = gain_ref[...]
    cell = jnp.sum(jnp.where(lane == patch, cell_ref[1], 0), axis=1, keepdims=True)
    picked = jnp.where(lane == cell, 1.0, 0.0)
    chosen = picked.astype(BF16)
    pgain = dot(picked, gain, HIGHEST)
    pshift = dot(pgain, inno[...], HIGHEST)
    ph, pl_ = split(-0.5 * pgain)
    for d in (1, 2, 3, 4, 5, 6, 7, 0):
        other = lax.rem(member + d, 8)
        at = columns(other)
        h, l = yh[:, at], yl[:, at]
        r = (dot(chosen, ah[:, at]) + dot(chosen, al[:, at])) + (pshift + (dot(ph, h) + (dot(ph, l) + dot(pl_, h))))
        rbuf[d] = r
        y_ref[1, 0:OBS, at] = r
        if d == 0:
            rows[1, member] = r
            continue
        copy = remote(rbuf.at[d], rows.at[1, member], asend_sem.at[d], arecv_sem.at[member], region, other)
        copy.start()
        sent.append(copy)
    shift = dot(gain, inno[...], HIGHEST)
    gh, gl = split(-0.5 * gain)
    for i in range(8):
        at = slice(i * 128, i * 128 + 128)
        h, l = yh[:, at], yl[:, at]
        x = x_ref[:, at] + (shift + (dot(gh, h) + (dot(gh, l) + dot(gl, h))))
        x2_ref[:, at] = x
        ah[:, at], al[:, at] = split(x)
    observed(1, patch, region, sides, nbr_ref, val_ref, var_ref, inno, var)
    for d in range(1, 8):
        other = lax.rem(member + d, 8)
        remote(rbuf.at[d], rows.at[1, other], asend_sem.at[d], arecv_sem.at[other], region, other).wait_recv()

    sent += exchange(1, picks, member, sides, rows, sbuf, y_ref, send_sem, recv_sem)

    def later_rows(s):
        await_side(1, s, member, sides, sbuf, y_ref, send_sem, recv_sem)

    border(1, later_rows, y_ref, yh, yl, ah, al, vinv, tref, wref, cross_ref, qref, inno, var)
    last_gain(vinv, wref, cross_ref, qref, gain_ref)
    gain = gain_ref[...]
    shift = dot(gain, inno[...], HIGHEST)
    gh, gl = split(-0.5 * gain)
    for d in (1, 2, 3, 4, 5, 6, 7, 0):
        other = lax.rem(member + d, 8)
        at = columns(other)
        h, l = yh[:, at], yl[:, at]
        x = x2_ref[:, at] + (shift + (dot(gh, h) + (dot(gh, l) + dot(gl, h))))
        if d == 0:
            o_ref[member] = x.T
            continue
        tbuf[d] = x.T
        copy = remote(tbuf.at[d], o_ref.at[member], osend_sem.at[d], orecv_sem.at[member], region, other)
        copy.start()
        sent.append(copy)
    for p in range(8):

        @pl.when(member != p)
        def _():
            remote(tbuf.at[1], o_ref.at[p], osend_sem.at[1], orecv_sem.at[p], region, p).wait_recv()

        out_ref[:, p, :] = o_ref[p]
    for copy in sent:
        copy.wait_send()


def on_device(state, neighbours, obs_cell, obs_values, obs_var):
    small = pltpu.VMEM((2, OBS, 256), F32)
    out = pl.pallas_call(
        whole_kernel,
        out_shape=jax.ShapeDtypeStruct((128, 8, 256), F32),
        in_specs=[ANY] * 4 + [SMEM],
        out_specs=VMEM,
        scratch_shapes=[
            pltpu.VMEM((128, 8, 256), F32),
            pltpu.VMEM((2, OBS, 256), jnp.int32),
            small,
            small,
            pltpu.VMEM((2, 8, OBS, 128), F32),
            pltpu.VMEM((2, 3, 8, 128, 128), F32),
            pltpu.VMEM((2, 384, 1024), F32),
            pltpu.VMEM((8, 256, 128), F32),
            pltpu.VMEM((256, 1024), F32),
            pltpu.VMEM((256, 1024), F32),
            pltpu.VMEM((8, OBS, 128), F32),
            pltpu.VMEM((8, 128, 256), F32),
            pltpu.VMEM((8, 128, 256), F32),
            pltpu.VMEM((384, 1024), BF16),
            pltpu.VMEM((384, 1024), BF16),
            pltpu.VMEM((256, 1024), BF16),
            pltpu.VMEM((256, 1024), BF16),
            pltpu.VMEM((3, 128, 128), F32),
            pltpu.VMEM((128, 128), F32),
            pltpu.VMEM((128, 256), F32),
            pltpu.VMEM((256, 384), F32),
            pltpu.VMEM((256, 256), F32),
            pltpu.VMEM((256, 384), F32),
            pltpu.VMEM((384, 128), F32),
            pltpu.VMEM((384, 128), F32),
            DMA((4,)),
            DMA((2, 3, 8)),
            DMA((2, 3, 8)),
            DMA((8,)),
            DMA((8,)),
            DMA((8,)),
            DMA((8,)),
            DMA((8,)),
            DMA((8,)),
        ],
        compiler_params=pltpu.CompilerParams(
            collective_id=0, has_side_effects=True, vmem_limit_bytes=60 * 1024 * 1024
        ),
        name="whole",
    )(
        state,
        jnp.transpose(obs_cell, (1, 2, 0)),
        jnp.transpose(obs_values, (1, 2, 0)),
        jnp.transpose(obs_var, (1, 2, 0)),
        jnp.transpose(neighbours, (1, 0)),
    )
    return out


def solution(mesh):
    in_specs = (P("member", "region", None), P(), P(), P(), P())
    out_specs = P("member", "region", None)
    return jax.shard_map(on_device, mesh=mesh, in_specs=in_specs, out_specs=out_specs, check_vma=False)
```

```python
import jax
import jax.numpy as jnp
from jax import lax
from jax.experimental import pallas as pl
from jax.experimental.pallas import tpu as pltpu
from jax.sharding import PartitionSpec as P

F32 = jnp.float32
BF16 = jnp.bfloat16
HIGHEST = lax.Precision.HIGHEST
MESH = pl.DeviceIdType.MESH
TILE = (8, 128)
OBS = 64
VMEM = pl.BlockSpec(memory_space=pltpu.VMEM)
SMEM = pl.BlockSpec(memory_space=pltpu.SMEM)
ANY = pl.BlockSpec(memory_space=pl.ANY)
DMA = pltpu.SemaphoreType.DMA


def dot(a, b, precision=None):
    return lax.dot_general(a, b, (((1,), (0,)), ((), ())), precision=precision, preferred_element_type=F32)


def dot_t(a, b, precision=None):
    return lax.dot_general(a, b, (((1,), (1,)), ((), ())), precision=precision, preferred_element_type=F32)


def split(x):
    high = x.astype(BF16)
    return high, (x - high.astype(F32)).astype(BF16)


def spread_tile(x):
    return jnp.broadcast_to(x, TILE)


def solve8(e, r):
    m = {}
    q = [None] * 8
    for i in range(0, 8, 2):
        a, b, d = e[i][i], e[i + 1][i], e[i + 1][i + 1]
        inv = 1.0 / (a * d - b * b)
        ai, bi, di = d * inv, b * inv, a * inv
        for k in range(i + 2, 8):
            m[k, i] = e[k][i] * ai - e[k][i + 1] * bi
            m[k, i + 1] = e[k][i + 1] * di - e[k][i] * bi
        for k in range(i + 2, 8):
            for j in range(i + 2, k + 1):
                e[k][j] = e[k][j] - (m[k, i] * e[j][i] + m[k, i + 1] * e[j][i + 1])
        for k in range(i + 2, 8):
            r[k] = r[k] - (m[k, i] * r[i] + m[k, i + 1] * r[i + 1])
        q[i], q[i + 1] = ai * r[i] - bi * r[i + 1], di * r[i + 1] - bi * r[i]
    for i in range(6, 0, -2):
        for k in range(i):
            q[k] = q[k] - (m[i, k] * q[i] + m[i + 1, k] * q[i + 1])
    return q


def inverse128(block):
    lane = lax.broadcasted_iota(jnp.int32, TILE, 1)
    sub = lax.broadcasted_iota(jnp.int32, TILE, 0)
    front = lax.broadcasted_iota(jnp.int32, (96, 128), 1) < 32

    def strip(_, matrix):
        tiles = [matrix[8 * i : 8 * i + 8, :] for i in range(4)]
        old = matrix[32:, :]
        for t in range(4):
            cols = [[spread_tile(tile[:, 8 * t + k : 8 * t + k + 1]) for k in range(8)] for tile in tiles]
            e = [[spread_tile(cols[t][j][k : k + 1, :]) if j <= k else None for j in range(8)] for k in range(8)]
            inside = (lane >= 8 * t) & (lane < 8 * t + 8)
            rows = [
                jnp.where(lane == 8 * t + k, 1.0, jnp.where(inside, 0.0, spread_tile(tiles[t][k : k + 1, :])))
                for k in range(8)
            ]
            new = solve8(e, rows)
            for i in range(4):
                if i == t:
                    u = new[0]
                    for k in range(1, 8):
                        u = jnp.where(sub == k, new[k], u)
                else:
                    p = [cols[i][k] * new[k] for k in range(8)]
                    u = jnp.where(inside, 0.0, tiles[i])
                    u = u - (((p[0] + p[1]) + (p[2] + p[3])) + ((p[4] + p[5]) + (p[6] + p[7])))
                tiles[i] = u
        top = jnp.concatenate(tiles, axis=0)
        padded = jnp.concatenate([top, jnp.zeros((96, 128), F32)], axis=0)
        fresh = jnp.where(front, 0.0, old) - dot(jnp.where(front, old, 0.0), padded, HIGHEST)
        return pltpu.roll(jnp.concatenate([fresh, top], axis=0), 96, 1)

    return lax.fori_loop(0, 4, strip, block)


def inverse128_unrolled(block):
    lane = lax.broadcasted_iota(jnp.int32, TILE, 1)
    sub = lax.broadcasted_iota(jnp.int32, TILE, 0)
    lanes = lax.broadcasted_iota(jnp.int32, (96, 128), 1)
    tiles = [block[8 * i : 8 * i + 8, :] for i in range(16)]
    for s in range(4):
        mine = list(range(4 * s, 4 * s + 4))
        others = [i for i in range(16) if i not in mine]
        old = jnp.concatenate([tiles[i] for i in others], axis=0)
        for t in mine:
            cols = {i: [spread_tile(tiles[i][:, 8 * t + k : 8 * t + k + 1]) for k in range(8)] for i in mine}
            e = [[spread_tile(cols[t][j][k : k + 1, :]) if j <= k else None for j in range(8)] for k in range(8)]
            inside = (lane >= 8 * t) & (lane < 8 * t + 8)
            rows = [
                jnp.where(lane == 8 * t + k, 1.0, jnp.where(inside, 0.0, spread_tile(tiles[t][k : k + 1, :])))
                for k in range(8)
            ]
            new = solve8(e, rows)
            for i in mine:
                if i == t:
                    u = new[0]
                    for k in range(1, 8):
                        u = jnp.where(sub == k, new[k], u)
                else:
                    u = jnp.where(inside, 0.0, tiles[i])
                    p = [cols[i][k] * new[k] for k in range(8)]
                    u = u - (((p[0] + p[1]) + (p[2] + p[3])) + ((p[4] + p[5]) + (p[6] + p[7])))
                tiles[i] = u
        low, high = 32 * s, 32 * s + 32
        parts = [jnp.concatenate([tiles[i] for i in mine], axis=0)]
        if low:
            parts.insert(0, jnp.zeros((low, 128), F32))
        if high < 128:
            parts.append(jnp.zeros((128 - high, 128), F32))
        strip = jnp.concatenate(parts, axis=0)
        inside = (lanes >= low) & (lanes < high)
        fresh = jnp.where(inside, 0.0, old) - dot(jnp.where(inside, old, 0.0), strip, HIGHEST)
        for q, i in enumerate(others):
            tiles[i] = fresh[8 * q : 8 * q + 8]
    return jnp.concatenate(tiles, axis=0)


def linked(nbr_ref, patch, home):
    first = last = first_at = last_at = jnp.int32(0)
    for j in range(5):
        n = nbr_ref[j, patch]
        here = (n >> 3) == home
        last = jnp.where(here, n, last)
        last_at = jnp.where(here, j, last_at)
    for j in reversed(range(5)):
        n = nbr_ref[j, patch]
        here = (n >> 3) == home
        first = jnp.where(here, n, first)
        first_at = jnp.where(here, j, first_at)
    return first, first_at, last, last_at


def place():
    region, member = lax.axis_index("region"), lax.axis_index("member")
    regions = lax.axis_size("region")
    sides = (region, lax.rem(region + 1, regions), lax.rem(region + regions - 1, regions))
    return region, member, sides


def columns(member):
    return pl.ds(pl.multiple_of(member * 128, 128), 128)


def all_peers(member, sides):
    return [
        {"region": sides[s], "member": lax.rem(member + d, 8)}
        for d in range(8)
        for s in range(3)
        if (s, d) != (0, 0)
    ]


def remote(src, dst, send, recv, region, member):
    return pltpu.make_async_remote_copy(
        src_ref=src,
        dst_ref=dst,
        send_sem=send,
        recv_sem=recv,
        device_id={"region": region, "member": member},
        device_id_type=MESH,
    )


def start_of(batch, s):
    return OBS if batch and s == 0 else 0


def exchange(batch, picks, member, sides, rows, sbuf, y_ref, send_sem, recv_sem):
    sent = []
    for s in range(3):
        start = start_of(batch, s)
        for d in range(8):
            other = lax.rem(member + d, 8)
            first, last = picks[s][d]
            if s == 0:
                if batch == 0:
                    sbuf[batch, s, d, 0:OBS, :] = rows[batch, other]
                sbuf[batch, s, d, OBS : 2 * OBS, :] = rows[batch, first]
            else:
                sbuf[batch, s, d, 0:OBS, :] = rows[batch, first]
                sbuf[batch, s, d, OBS : 2 * OBS, :] = rows[batch, last]
            if s == 0 and d == 0:
                y_ref[batch, start : 2 * OBS, columns(member)] = sbuf[batch, 0, 0, start : 2 * OBS, :]
                continue
            copy = remote(
                sbuf.at[batch, s, d, pl.ds(start, 2 * OBS - start)],
                y_ref.at[batch, pl.ds(s * 128 + start, 2 * OBS - start), columns(member)],
                send_sem.at[batch, s, d],
                recv_sem.at[batch, s, member],
                sides[s],
                other,
            )
            copy.start()
            sent.append(copy)
    return sent


def await_side(batch, s, member, sides, sbuf, y_ref, send_sem, recv_sem):
    start = start_of(batch, s)
    for d in range(8):
        if (s, d) == (0, 0):
            continue
        other = lax.rem(member + d, 8)
        remote(
            sbuf.at[batch, s, d, pl.ds(start, 2 * OBS - start)],
            y_ref.at[batch, pl.ds(s * 128 + start, 2 * OBS - start), columns(other)],
            send_sem.at[batch, s, d],
            recv_sem.at[batch, s, other],
            sides[s],
            other,
        ).wait_recv()


def observed(batch, patch, region, sides, nbr_ref, val_ref, var_ref, inno, var):
    lane = lax.broadcasted_iota(jnp.int32, (OBS, 256), 1)
    same, same_at, _, _ = linked(nbr_ref, patch, region)
    slots = [(patch, jnp.int32(-1)), (same, same_at)]
    for side in (sides[2], sides[1]):
        f, fa, l, la = linked(nbr_ref, patch, side)
        slots += [(f, fa), (l, la)]
    for i, (n, at) in enumerate(slots):
        here = lane == n
        value = jnp.sum(jnp.where(here, val_ref[batch], 0.0), axis=1, keepdims=True)
        noise = jnp.sum(jnp.where(here, var_ref[batch], 0.0), axis=1, keepdims=True)
        widening = (at + 2).astype(F32)
        inno[i * OBS : (i + 1) * OBS, :] = jnp.broadcast_to(value, (OBS, 128))
        var[i * OBS : (i + 1) * OBS, :] = jnp.broadcast_to(noise * widening, (OBS, 128))


def border(batch, await_rows, y_ref, yh, yl, ah, al, vinv, tref, wref, cross_ref, qref, inno, var):
    corner = lax.broadcasted_iota(jnp.int32, (128, 128), 0) == lax.broadcasted_iota(jnp.int32, (128, 128), 1)
    inverse = inverse128_unrolled if batch else inverse128
    for s in range(3):
        at = slice(128 * s, 128 * s + 128)
        await_rows(s)

        def centre(i, _):
            rows = pl.ds(pl.multiple_of(s * 128 + i * 32, 32), 32)
            y = y_ref[batch, rows, :]
            mean = jnp.sum(y, axis=1, keepdims=True) * (1.0 / 1024.0)
            yh[rows, :], yl[rows, :] = split(y - mean)
            inno[rows, :] = inno[rows, :] - mean
            return 0

        lax.fori_loop(0, 4, centre, 0)
        high, low = yh[at, :], yl[at, :]
        upto = slice(0, 128 * s + 128)
        total = dot_t(high, yh[upto, :]) + (dot_t(high, yl[upto, :]) + dot_t(low, yh[upto, :]))
        c = [total[:, 128 * i : 128 * i + 128] * (1.0 / 1023.0) for i in range(s + 1)]
        schur = c[s] + jnp.where(corner, var[at, :], 0.0)
        if batch:
            x = cross_of(ah, al, high, low)
        if s == 0:
            if batch:
                cross_ref[:, 0:128] = x
            vinv[0] = inverse(schur)
        elif s == 1:
            t10 = dot(c[0], vinv[0], HIGHEST)
            tref[...] = t10
            schur = schur - dot_t(t10, c[0], HIGHEST)
            if batch:
                cross_ref[:, 128:256] = x - dot_t(cross_ref[:, 0:128], t10, HIGHEST)
            vinv[1] = inverse(schur)
            if batch:
                p1 = dot(cross_ref[:, 128:256], vinv[1], HIGHEST)
                qref[:, 128:256] = p1
                qref[:, 0:128] = dot(cross_ref[:, 0:128], vinv[0], HIGHEST) - dot(p1, t10, HIGHEST)
        else:
            t10 = tref[...]
            t20 = dot(c[0], vinv[0], HIGHEST)
            e21 = c[1] - dot_t(c[0], t10, HIGHEST)
            t21 = dot(e21, vinv[1], HIGHEST)
            schur = schur - (dot_t(t20, c[0], HIGHEST) + dot_t(t21, e21, HIGHEST))
            wref[:, 0:128] = t20 - dot(t21, t10, HIGHEST)
            wref[:, 128:256] = t21
            if batch:
                past = dot_t(cross_ref[:, 0:128], t20, HIGHEST) + dot_t(cross_ref[:, 128:256], t21, HIGHEST)
                cross_ref[:, 256:384] = x - past
            vinv[2] = inverse(schur)


def cross_of(ah, al, high, low):
    a, b = ah[...], al[...]
    return (dot_t(a, high) + (dot_t(a, low) + dot_t(b, high))) * (1.0 / 1023.0)


def whole_gain(cross, vinv, tref, wref, gain_ref):
    x0, x1, x2 = (cross[:, 128 * i : 128 * i + 128] for i in range(3))
    t10, w0, w1 = tref[...], wref[:, 0:128], wref[:, 128:256]
    x1 = x1 - dot_t(x0, t10, HIGHEST)
    x2 = x2 - (dot_t(x0, w0, HIGHEST) + dot_t(cross[:, 128:256], w1, HIGHEST))
    p0, p1 = dot(x0, vinv[0], HIGHEST), dot(x1, vinv[1], HIGHEST)
    last = dot(x2, vinv[2], HIGHEST)
    gain_ref[:, 256:384] = last
    gain_ref[:, 128:256] = p1 - dot(last, w1, HIGHEST)
    gain_ref[:, 0:128] = (p0 - dot(p1, t10, HIGHEST)) - dot(last, w0, HIGHEST)


def last_gain(vinv, wref, cross_ref, qref, gain_ref):
    last = dot(cross_ref[:, 256:384], vinv[2], HIGHEST)
    gain_ref[:, 256:384] = last
    gain_ref[:, 0:256] = qref[...] - dot(last, wref[...], HIGHEST)


def whole_kernel(
    state_hbm, cell_hbm, val_hbm, var_hbm, nbr_ref, out_ref,
    state_ref, cell_ref, val_ref, var_ref,
    rows, sbuf, y_ref, xbuf, x_ref, x2_ref, rbuf, tbuf, o_ref,
    yh, yl, ah, al, vinv, tref, wref, cross_ref, qref, gain_ref, inno, var,
    load_sem, send_sem, recv_sem, xsend_sem, xrecv_sem, asend_sem, arecv_sem, osend_sem, orecv_sem,
):
    region, member, sides = place()
    patch = region * 8 + member
    lane = lax.broadcasted_iota(jnp.int32, (OBS, 256), 1)
    loads = [
        pltpu.make_async_copy(src, dst, load_sem.at[i])
        for i, (src, dst) in enumerate(
            ((state_hbm, state_ref), (cell_hbm, cell_ref), (val_hbm, val_ref), (var_hbm, var_ref))
        )
    ]
    for load in loads:
        load.start()
    peers = all_peers(member, sides)
    barrier = pltpu.get_barrier_semaphore()
    for peer in peers:
        pl.semaphore_signal(barrier, inc=1, device_id=peer, device_id_type=MESH)
    picks = [[], [], []]
    for s in range(3):
        for d in range(8):
            first, _, last, _ = linked(nbr_ref, sides[s] * 8 + lax.rem(member + d, 8), region)
            picks[s].append((first & 7, last & 7))
    loads[0].wait()
    loads[1].wait()
    for q in range(8):
        cell = jnp.sum(jnp.where(lane == region * 8 + q, cell_ref[0], 0), axis=1, keepdims=True)
        picked = jnp.where(lane == cell, 1.0, 0.0)
        chosen, x = picked.astype(BF16), state_ref[:, q, :]
        high = x.astype(BF16)
        middle, low = split(x - high.astype(F32))
        rows[0, q] = (dot_t(chosen, high) + dot_t(chosen, middle)) + dot_t(chosen, low)
    pl.semaphore_wait(barrier, len(peers))

    sent = exchange(0, picks, member, sides, rows, sbuf, y_ref, send_sem, recv_sem)
    for q in range(8):
        xbuf[q] = state_ref[:, q, :].T
    for d in range(1, 8):
        other = lax.rem(member + d, 8)
        copy = remote(xbuf.at[other], x_ref.at[:, columns(member)], xsend_sem.at[d], xrecv_sem.at[member], region, other)
        copy.start()
        sent.append(copy)
    x_ref[:, columns(member)] = xbuf[member]
    loads[2].wait()
    loads[3].wait()
    observed(0, patch, region, sides, nbr_ref, val_ref, var_ref, inno, var)

    def first_rows(s):
        await_side(0, s, member, sides, sbuf, y_ref, send_sem, recv_sem)

    border(0, first_rows, y_ref, yh, yl, ah, al, vinv, tref, wref, cross_ref, qref, inno, var)
    for d in range(8):
        other = lax.rem(member + 8 - d, 8)
        at = columns(other)
        if d:
            remote(xbuf.at[other], x_ref.at[:, at], xsend_sem.at[d], xrecv_sem.at[other], region, other).wait_recv()
        high, low = split(x_ref[:, at])
        ah[:, at], al[:, at] = high, low
        part = dot_t(high, yh[:, at]) + (dot_t(high, yl[:, at]) + dot_t(low, yh[:, at]))
        cross_ref[...] = cross_ref[...] + part if d else part

    whole_gain(cross_ref[...] * (1.0 / 1023.0), vinv, tref, wref, gain_ref)
    gain = gain_ref[...]
    cell = jnp.sum(jnp.where(lane == patch, cell_ref[1], 0), axis=1, keepdims=True)
    picked = jnp.where(lane == cell, 1.0, 0.0)
    chosen = picked.astype(BF16)
    pgain = dot(picked, gain, HIGHEST)
    pshift = dot(pgain, inno[...], HIGHEST)
    ph, pl_ = split(-0.5 * pgain)
    for d in (1, 2, 3, 4, 5, 6, 7, 0):
        other = lax.rem(member + d, 8)
        at = columns(other)
        h, l = yh[:, at], yl[:, at]
        r = (dot(chosen, ah[:, at]) + dot(chosen, al[:, at])) + (pshift + (dot(ph, h) + (dot(ph, l) + dot(pl_, h))))
        rbuf[d] = r
        y_ref[1, 0:OBS, at] = r
        if d == 0:
            rows[1, member] = r
            continue
        copy = remote(rbuf.at[d], rows.at[1, member], asend_sem.at[d], arecv_sem.at[member], region, other)
        copy.start()
        sent.append(copy)
    shift = dot(gain, inno[...], HIGHEST)
    gh, gl = split(-0.5 * gain)
    for i in range(8):
        at = slice(i * 128, i * 128 + 128)
        h, l = yh[:, at], yl[:, at]
        x = x_ref[:, at] + (shift + (dot(gh, h) + (dot(gh, l) + dot(gl, h))))
        x2_ref[:, at] = x
        ah[:, at], al[:, at] = split(x)
    observed(1, patch, region, sides, nbr_ref, val_ref, var_ref, inno, var)
    for d in range(1, 8):
        other = lax.rem(member + d, 8)
        remote(rbuf.at[d], rows.at[1, other], asend_sem.at[d], arecv_sem.at[other], region, other).wait_recv()

    sent += exchange(1, picks, member, sides, rows, sbuf, y_ref, send_sem, recv_sem)

    def later_rows(s):
        await_side(1, s, member, sides, sbuf, y_ref, send_sem, recv_sem)

    border(1, later_rows, y_ref, yh, yl, ah, al, vinv, tref, wref, cross_ref, qref, inno, var)
    last_gain(vinv, wref, cross_ref, qref, gain_ref)
    gain = gain_ref[...]
    shift = dot(gain, inno[...], HIGHEST)
    gh, gl = split(-0.5 * gain)
    for d in (1, 2, 3, 4, 5, 6, 7, 0):
        other = lax.rem(member + d, 8)
        at = columns(other)
        h, l = yh[:, at], yl[:, at]
        x = x2_ref[:, at] + (shift + (dot(gh, h) + (dot(gh, l) + dot(gl, h))))
        if d == 0:
            o_ref[member] = x.T
            continue
        tbuf[d] = x.T
        copy = remote(tbuf.at[d], o_ref.at[member], osend_sem.at[d], orecv_sem.at[member], region, other)
        copy.start()
        sent.append(copy)
    for p in range(8):

        @pl.when(member != p)
        def _():
            remote(tbuf.at[1], o_ref.at[p], osend_sem.at[1], orecv_sem.at[p], region, p).wait_recv()

        out_ref[:, p, :] = o_ref[p]
    for copy in sent:
        copy.wait_send()


def on_device(state, neighbours, obs_cell, obs_values, obs_var):
    small = pltpu.VMEM((2, OBS, 256), F32)
    out = pl.pallas_call(
        whole_kernel,
        out_shape=jax.ShapeDtypeStruct((128, 8, 256), F32),
        in_specs=[ANY] * 4 + [SMEM],
        out_specs=VMEM,
        scratch_shapes=[
            pltpu.VMEM((128, 8, 256), F32),
            pltpu.VMEM((2, OBS, 256), jnp.int32),
            small,
            small,
            pltpu.VMEM((2, 8, OBS, 128), F32),
            pltpu.VMEM((2, 3, 8, 128, 128), F32),
            pltpu.VMEM((2, 384, 1024), F32),
            pltpu.VMEM((8, 256, 128), F32),
            pltpu.VMEM((256, 1024), F32),
            pltpu.VMEM((256, 1024), F32),
            pltpu.VMEM((8, OBS, 128), F32),
            pltpu.VMEM((8, 128, 256), F32),
            pltpu.VMEM((8, 128, 256), F32),
            pltpu.VMEM((384, 1024), BF16),
            pltpu.VMEM((384, 1024), BF16),
            pltpu.VMEM((256, 1024), BF16),
            pltpu.VMEM((256, 1024), BF16),
            pltpu.VMEM((3, 128, 128), F32),
            pltpu.VMEM((128, 128), F32),
            pltpu.VMEM((128, 256), F32),
            pltpu.VMEM((256, 384), F32),
            pltpu.VMEM((256, 256), F32),
            pltpu.VMEM((256, 384), F32),
            pltpu.VMEM((384, 128), F32),
            pltpu.VMEM((384, 128), F32),
            DMA((4,)),
            DMA((2, 3, 8)),
            DMA((2, 3, 8)),
            DMA((8,)),
            DMA((8,)),
            DMA((8,)),
            DMA((8,)),
            DMA((8,)),
            DMA((8,)),
        ],
        compiler_params=pltpu.CompilerParams(
            collective_id=0, has_side_effects=True, vmem_limit_bytes=60 * 1024 * 1024
        ),
        name="whole",
    )(
        state,
        jnp.transpose(obs_cell, (1, 2, 0)),
        jnp.transpose(obs_values, (1, 2, 0)),
        jnp.transpose(obs_var, (1, 2, 0)),
        jnp.transpose(neighbours, (1, 0)),
    )
    return out


def solution(mesh):
    in_specs = (P("member", "region", None), P(), P(), P(), P())
    out_specs = P("member", "region", None)
    return jax.shard_map(on_device, mesh=mesh, in_specs=in_specs, out_specs=out_specs, check_vma=False)
```
